32 devices in a mesh: row: 16 (over z, y, core), col: 2 (over x).
Axes of the slice: x: 2, y: 2, z: 4, core: 2. Of those that a mesh axis runs over, the one named last changes fastest.
Arguments:
- pair: bfloat16 [384, 384, 128], P('row', 'col'), may hold values from -6 to 6
- gain: float32 [128], replicated, may hold values from 0.1 to 1.9
- projections: bfloat16 [5, 128, 128], replicated, may hold values from -0.5 to 0.5
- bias_weight: bfloat16 [128, 4], replicated, as said below
- valid_len: int32 [1], replicated, may hold values from 192 to 384
- out_cotangent: bfloat16 [384, 384, 128], P('row', 'col'), may hold values from -6 to 6
Outputs:
- attended: bfloat16 [384, 384, 128], P('row', 'col')
- pair_gradient: float32 [384, 384, 128], P('row', 'col')
- projection_grad: float32 [5, 128, 128], replicated
- bias_weight_grad: float32 [128, 4], replicated
- gain_gradient: float32 [128], replicated
The draws below stay inside these ranges and needn't reach their ends.
Inputs may be any that keep to these rules, and one draw needn't show every extreme that they name: `bias_weight`: scale of the bias projection entries is free; rows are drawn independently.
All inputs are finite; a program needn't handle non-finite values.
Results may differ from the reference program's by a relative error of at most 0.0045.
The reference program's roundings to bfloat16 on the way count: a program that leaves them out, or rounds other values in their place, can miss the bound.
Values may be sent and summed in bfloat16 or wider, within the bound.
A program may use at most 64 MiB of HBM per device.

```python
import jax
import jax.numpy as jnp
from jax import lax

C = 128
H = 4
QB = 384
N = 384


def draw_bias_weight(key, part):
    base = jax.random.normal(jax.random.fold_in(key, 17), (C, H), jnp.float32) * C ** (-0.5)
    return base.astype(jnp.bfloat16)


def level_of(stream_key, shape, pieces, low, high):
    def one(position, shards_of):
        steps = jax.random.uniform(jax.random.fold_in(jax.random.fold_in(stream_key, 6), position), (shards_of,), jnp.float32, low / len(pieces), high / len(pieces))
        return jnp.repeat(jnp.exp(steps), shape[position] // shards_of).reshape((-1,) + (1,) * (len(shape) - position - 1))

    factor_of = one(*pieces[0])
    for cut in pieces[1:]:
        factor_of = factor_of * one(*cut)
    return factor_of


def normal_values(rng, shape, deviation, limit, pieces=(), kind=jnp.bfloat16):
    factor_of = level_of(rng, shape, pieces, -0.22, 0.18) if pieces else 1.0
    array = jax.random.normal(rng, shape, jnp.float32) * deviation * factor_of
    return jnp.minimum(jnp.maximum(array, -limit), limit).astype(kind)


def setup_inputs(seed: int = 0) -> dict:
    key_list = jax.random.split(jax.random.key(seed), 7)
    pair = normal_values(key_list[0], (N, N, C), 1.0, 6.0, ((0, 16), (1, 2)))
    gain = jnp.clip(1.0 + 0.18 * jax.random.normal(key_list[1], (C,), jnp.float32), 0.1, 1.9)
    projections = normal_values(key_list[2], (5, C, C), C ** -0.5, 0.5)
    bias_weight = draw_bias_weight(jax.random.fold_in(key_list[6], 71), 0)
    valid_len = jax.random.randint(key_list[4], (1,), N // 2, N + 1).astype(jnp.int32)
    out_cotangent = normal_values(key_list[5], (N, N, C), 1.0, 6.0, ((0, 16), (1, 2)))
    return dict(pair=pair, gain=gain, projections=projections, bias_weight=bias_weight, valid_len=valid_len, out_cotangent=out_cotangent)


EPS = 1e-05

def dense(left, right):
    return jnp.einsum('abc,cd->abd', left.astype(jnp.float32), right.astype(jnp.float32))

def outer_sum(left, right):
    return jnp.einsum('abc,abd->cd', left.astype(jnp.float32), right.astype(jnp.float32))

def attend_forward(query, key, value, bias_blocks, keep):
    ncols, rows, heads, width = query.shape
    nblocks = bias_blocks.shape[0]
    scale = width ** (-0.5)

    def per_column(cols):
        qcol, kcol, vcol = cols

        def per_block(blk):
            qblk, bblk = blk
            scores = jnp.einsum('qhd,khd->hqk', qblk.astype(jnp.float32), kcol.astype(jnp.float32)) * scale + bblk.astype(jnp.float32)
            scores = jnp.where(keep[None, None, :], scores, -1000000000.0)
            probs = jax.nn.softmax(scores, axis=-1)
            out = jnp.einsum('hqk,khd->qhd', probs.astype(jnp.bfloat16).astype(jnp.float32), vcol.astype(jnp.float32))
            return out.astype(jnp.bfloat16)
        return lax.map(per_block, (qcol.reshape(nblocks, rows // nblocks, heads, width), bias_blocks)).reshape(rows, heads, width)
    return lax.map(per_column, (query, key, value))

def attend_backward(query, key, value, d_context, bias_blocks, keep):
    ncols, rows, heads, width = query.shape
    nblocks = bias_blocks.shape[0]
    qsize = rows // nblocks
    scale = width ** (-0.5)

    def per_column(total, cols):
        qcol, kcol, vcol, dcol = cols

        def per_block(carry, blk):
            dk_acc, dv_acc = carry
            qblk, dblk, bblk = blk
            scores = jnp.einsum('qhd,khd->hqk', qblk.astype(jnp.float32), kcol.astype(jnp.float32)) * scale + bblk.astype(jnp.float32)
            scores = jnp.where(keep[None, None, :], scores, -1000000000.0)
            probs = jax.nn.softmax(scores, axis=-1)
            weights_b = probs.astype(jnp.bfloat16).astype(jnp.float32)
            d_probs = jnp.einsum('qhd,khd->hqk', dblk.astype(jnp.float32), vcol.astype(jnp.float32))
            d_scores = probs * (d_probs - lax.optimization_barrier(jnp.sum(probs * d_probs, axis=-1, keepdims=True)))
            dsb = d_scores.astype(jnp.bfloat16).astype(jnp.float32)
            dq = (jnp.einsum('hqk,khd->qhd', dsb, kcol.astype(jnp.float32)) * scale).astype(jnp.bfloat16)
            dk_acc = dk_acc + jnp.einsum('hqk,qhd->khd', dsb, qblk.astype(jnp.float32)) * scale
            dv_acc = dv_acc + jnp.einsum('hqk,qhd->khd', weights_b, dblk.astype(jnp.float32))
            return ((dk_acc, dv_acc), (dq, d_scores))
        zeros = jnp.zeros((rows, heads, width), jnp.float32)
        (dk, dv), (dq, dscores) = lax.scan(per_block, (zeros, zeros), (qcol.reshape(nblocks, qsize, heads, width), dcol.reshape(nblocks, qsize, heads, width), bias_blocks))
        return (total + dscores, (dq.reshape(rows, heads, width), dk.astype(jnp.bfloat16), dv.astype(jnp.bfloat16)))
    start = jnp.zeros(bias_blocks.shape, jnp.float32)
    total, (dq, dk, dv) = lax.scan(per_column, start, (query, key, value, d_context))
    return (dq, dk, dv, total)

def reference(pair, gain, projections, bias_weight, valid_len, out_cotangent):
    heads = bias_weight.shape[1]
    width = pair.shape[2] // heads
    rows = pair.shape[0]
    pair_float = pair.astype(jnp.float32)
    average_value = lax.optimization_barrier(jnp.mean(pair_float, axis=-1, keepdims=True))
    var = lax.optimization_barrier(jnp.mean((pair_float - average_value) ** 2, axis=-1, keepdims=True))
    inverse_deviation = lax.rsqrt(var + EPS)
    centered_scaled = (pair_float - average_value) * inverse_deviation
    normalized_pair = (centered_scaled * gain).astype(jnp.bfloat16)
    query = dense(normalized_pair, projections[0]).astype(jnp.bfloat16)
    key = dense(normalized_pair, projections[1]).astype(jnp.bfloat16)
    value = dense(normalized_pair, projections[2]).astype(jnp.bfloat16)
    gate = jax.nn.sigmoid(dense(normalized_pair, projections[3]))
    pair_bias = dense(normalized_pair, bias_weight)
    bias_t = jnp.transpose(pair_bias, (2, 1, 0))
    bias_blocks = bias_t.reshape(heads, rows // QB, QB, rows).transpose(1, 0, 2, 3)
    keep = jnp.arange(rows, dtype=jnp.int32) < valid_len[0]

    def split(tensor):
        return jnp.moveaxis(tensor, 1, 0).reshape(rows, rows, heads, width)

    def join(tensor):
        return jnp.moveaxis(tensor.reshape(rows, rows, heads * width), 0, 1)
    context = join(attend_forward(split(query), split(key), split(value), bias_blocks, keep))
    gated = (gate * context.astype(jnp.float32)).astype(jnp.bfloat16)
    attended = dense(gated, projections[4]).astype(jnp.bfloat16)
    d_gated = dense(out_cotangent, projections[4].T)
    d_context = (d_gated * gate).astype(jnp.bfloat16)
    d_gate_pre = (d_gated * context.astype(jnp.float32) * gate * (1.0 - gate)).astype(jnp.bfloat16)
    dq, dk, dv, total = attend_backward(split(query), split(key), split(value), split(d_context), bias_blocks, keep)
    dq, dk, dv = (join(dq), join(dk), join(dv))
    d_bias_t = total.transpose(1, 0, 2, 3).reshape(heads, rows, rows)
    d_bias = jnp.transpose(d_bias_t, (2, 1, 0)).astype(jnp.bfloat16)
    normalized_gradient = dense(dq, projections[0].T) + dense(dk, projections[1].T) + dense(dv, projections[2].T)
    normalized_gradient = normalized_gradient + dense(d_gate_pre, projections[3].T) + dense(d_bias, bias_weight.T)
    projection_grad = jnp.stack([outer_sum(normalized_pair, dq), outer_sum(normalized_pair, dk), outer_sum(normalized_pair, dv), outer_sum(normalized_pair, d_gate_pre), outer_sum(gated, out_cotangent)])
    bias_weight_grad = outer_sum(normalized_pair, d_bias)
    gain_gradient = lax.optimization_barrier(jnp.sum(normalized_gradient * centered_scaled, axis=(0, 1)))
    scaled_output = normalized_gradient * gain
    pair_gradient = inverse_deviation * (scaled_output - lax.optimization_barrier(jnp.mean(scaled_output, axis=-1, keepdims=True)) - centered_scaled * lax.optimization_barrier(jnp.mean(scaled_output * centered_scaled, axis=-1, keepdims=True)))
    return (attended, pair_gradient, projection_grad, bias_weight_grad, gain_gradient)
```

```python
import functools

import jax
import jax.numpy as jnp
from jax import lax
from jax.experimental import pallas as pl
from jax.experimental.pallas import tpu as pltpu
from jax.sharding import PartitionSpec as P

EPS = 1e-05
F32 = jnp.float32
BF16 = jnp.bfloat16


def mm(left, right):
    return lax.dot_general(left, right, (((1,), (0,)), ((), ())), preferred_element_type=F32)


def mm_nt(left, right):
    return lax.dot_general(left, right, (((1,), (1,)), ((), ())), preferred_element_type=F32)


def attention_kernel(
    heads, valid_ref, x_ref, cot_ref, w_in_ref, w_out_ref, bias_ref,
    att_ref, dn_ref, dbias_ref, parts_ref, bias_s, dbias_s,
):
    step = pl.program_id(0)
    _, n_row, tile_rows, channels = x_ref.shape
    n_col, tile_cols = bias_ref.shape[1], bias_ref.shape[4]
    rows = n_row * tile_rows
    width = channels // heads
    scale = width ** (-0.5)
    keep_lanes = lax.broadcasted_iota(jnp.int32, (rows, 1), 0) < valid_ref[0]

    @pl.when(step == 0)
    def _():
        for h in range(heads):
            for c in range(n_col):
                block = bias_ref[:, c, h].reshape(rows, tile_cols)
                bias_s[h, :, c * tile_cols : (c + 1) * tile_cols] = jnp.where(
                    keep_lanes, block, -1000000000.0
                )
        dbias_s[...] = jnp.zeros_like(dbias_s)
        parts_ref[...] = jnp.zeros_like(parts_ref)

    x = x_ref[0].astype(F32).reshape(rows, channels).astype(BF16)
    cot = cot_ref[0].astype(F32).reshape(rows, channels).astype(BF16)
    proj = mm(x, w_in_ref[...])
    query = proj[:, :channels].astype(BF16)
    key_f = jnp.where(keep_lanes, proj[:, channels : 2 * channels], 0.0)
    key = key_f.astype(BF16)
    value_f = proj[:, 2 * channels : 3 * channels]
    value = value_f.astype(BF16)
    gate = jax.nn.sigmoid(proj[:, 3 * channels :])
    d_gated = mm_nt(cot, w_out_ref[...])
    d_context_f = d_gated * gate
    d_context = d_context_f.astype(BF16)
    key_t = jnp.transpose(key_f).astype(BF16)
    value_t = jnp.transpose(value_f).astype(BF16)
    lane_head = lax.broadcasted_iota(jnp.int32, (rows, channels), 1) // width
    ctx_parts, dq_parts = [], []
    dk = jnp.zeros((rows, channels), F32)
    dv = jnp.zeros((rows, channels), F32)
    for h in range(heads):
        mine = lane_head == h
        q_h = jnp.where(mine, query, jnp.zeros_like(query))
        dc_h = jnp.where(mine, d_context, jnp.zeros_like(d_context))
        s = mm_nt(key, q_h) * scale + bias_s[h]
        e = jnp.exp(s - jnp.max(s, axis=0, keepdims=True))
        p = e * (1.0 / jnp.sum(e, axis=0, keepdims=True))
        d_p = mm_nt(value, dc_h)
        delta = jnp.sum(p * d_p, axis=0, keepdims=True)
        ds = p * (d_p - delta)
        dbias_s[h] += ds
        p_b = p.astype(BF16)
        ds_b = ds.astype(BF16)
        ctx_parts.append(mm(value_t[h * width : (h + 1) * width], p_b))
        dq_parts.append(mm(key_t[h * width : (h + 1) * width], ds_b))
        dv += mm(p_b, dc_h)
        dk += mm(ds_b, q_h)
    context = jnp.transpose(jnp.concatenate(ctx_parts, axis=0)).astype(BF16).astype(F32)
    dq = (jnp.transpose(jnp.concatenate(dq_parts, axis=0)) * scale).astype(BF16)
    dk = (dk * scale).astype(BF16)
    dv = dv.astype(BF16)
    gated_f = gate * context
    gated = gated_f.astype(BF16)
    att = mm(gated, w_out_ref[...])
    att_ref[0] = att.reshape(n_row, tile_rows, channels).astype(att_ref.dtype)
    d_gate = (d_gated * context * gate * (1.0 - gate)).astype(BF16)
    grads = jnp.concatenate([dq, dk, dv, d_gate], axis=1)
    dn = mm_nt(grads, w_in_ref[...])
    dn_ref[0] = dn.reshape(n_row, tile_rows, channels).astype(dn_ref.dtype)
    x_t = jnp.transpose(x.astype(F32)).astype(BF16)
    parts_ref[:, : 4 * channels] += mm(x_t, grads)
    gated_t = jnp.transpose(gated.astype(F32)).astype(BF16)
    parts_ref[:, 4 * channels :] += mm(gated_t, cot)

    @pl.when(step == pl.num_programs(0) - 1)
    def _():
        for h in range(heads):
            for c in range(n_col):
                block = dbias_s[h, :, c * tile_cols : (c + 1) * tile_cols]
                dbias_ref[:, c, h] = block.reshape(n_row, tile_rows, tile_cols)


def attention(valid_len, x_cols, cot_cols, w_in, w_out, bias):
    ncols, n_row, tile_rows, channels = x_cols.shape
    heads, n_col, tile_cols = bias.shape[2], bias.shape[1], bias.shape[4]
    rows = n_row * tile_rows
    column = pl.BlockSpec((1, n_row, tile_rows, channels), lambda j: (j, 0, 0, 0))

    def whole(shape):
        return pl.BlockSpec(shape, lambda j: (0,) * len(shape))

    return pl.pallas_call(
        functools.partial(attention_kernel, heads),
        grid=(ncols,),
        in_specs=[
            pl.BlockSpec(memory_space=pltpu.SMEM),
            column,
            column,
            whole(w_in.shape),
            whole(w_out.shape),
            whole(bias.shape),
        ],
        out_specs=[column, column, whole(bias.shape), whole((channels, 5 * channels))],
        out_shape=[
            jax.ShapeDtypeStruct(x_cols.shape, BF16),
            jax.ShapeDtypeStruct(x_cols.shape, BF16),
            jax.ShapeDtypeStruct(bias.shape, F32),
            jax.ShapeDtypeStruct((channels, 5 * channels), F32),
        ],
        scratch_shapes=[
            pltpu.VMEM((heads, rows, rows), F32),
            pltpu.VMEM((heads, rows, rows), F32),
        ],
        compiler_params=pltpu.CompilerParams(
            dimension_semantics=("arbitrary",), vmem_limit_bytes=60 * 1024 * 1024
        ),
    )(valid_len, x_cols, cot_cols, w_in, w_out, bias)


MESH = pl.DeviceIdType.MESH
VM = pltpu.VMEM
DMA = pltpu.SemaphoreType.DMA


def place():
    row, col = lax.axis_index("row"), lax.axis_index("col")
    return row, col, row // 4, lax.rem(row // 2, 2), lax.rem(row, 2)


def meet_all():
    row, col = lax.axis_index("row"), lax.axis_index("col")
    n_row, n_col = lax.axis_size("row"), lax.axis_size("col")
    barrier = pltpu.get_barrier_semaphore()

    def greet(i, carry):
        there = (lax.rem(row + i // n_col, n_row), lax.rem(col + lax.rem(i, n_col), n_col))
        pl.semaphore_signal(barrier, inc=1, device_id=there, device_id_type=MESH)
        return carry

    lax.fori_loop(1, n_row * n_col, greet, 0)
    pl.semaphore_wait(barrier, n_row * n_col - 1)


def push(src, dst, send, recv, where):
    pltpu.make_async_remote_copy(
        src_ref=src, dst_ref=dst, send_sem=send, recv_sem=recv,
        device_id=where, device_id_type=MESH,
    ).start()


def await_bytes(ref, sem):
    pltpu.make_async_copy(ref, ref, sem).wait()


def mates(n_col, mid, col):
    for i in range(1, 2 * n_col):
        yield i - 1, lax.rem(mid + i // n_col, 2), lax.rem(col + i % n_col, n_col)


def gather_kernel(
    x_ref, cot_ref, bias_ref, xo_ref, coto_ref, biaso_ref,
    s_aa, r_aa, s_out, r_out, s_mate, r_mate, s_core, r_core, s_loc,
):
    row, col, outer, mid, core = place()
    n_row, ncols = x_ref.shape[:2]
    n_out, _, _, n_col = biaso_ref.shape[:4]
    meet_all()
    for i in range(1, n_out):
        there = lax.rem(outer + i, n_out) * 4 + mid * 2 + core
        push(bias_ref, biaso_ref.at[outer, mid, core, col], s_out.at[i - 1], r_out.at[i - 1], (there, col))
    local = [
        pltpu.make_async_copy(bias_ref, biaso_ref.at[outer, mid, core, col], s_loc.at[0]),
        pltpu.make_async_copy(x_ref.at[row], xo_ref.at[:, row], s_loc.at[1]),
        pltpu.make_async_copy(cot_ref.at[row], coto_ref.at[:, row], s_loc.at[2]),
    ]
    for copy in local:
        copy.start()

    def columns(c, carry):
        def peer(i, carry):
            r = lax.rem(row + i, n_row)
            push(x_ref.at[r, c], xo_ref.at[c, row], s_aa.at[0], r_aa.at[0, c], (r, col))
            push(cot_ref.at[r, c], coto_ref.at[c, row], s_aa.at[1], r_aa.at[1, c], (r, col))
            return carry

        return lax.fori_loop(1, n_row, peer, carry)

    split = (ncols + 1) // 2
    lax.fori_loop(0, split, columns, 0)
    for copy in local:
        copy.wait()
    for i in range(1, n_out):
        await_bytes(bias_ref, s_out.at[i - 1])
        await_bytes(bias_ref, r_out.at[i - 1])
    mine = biaso_ref.at[:, mid, core, col]
    for i, m, k in mates(n_col, mid, col):
        push(mine, mine, s_mate.at[i], r_mate.at[i], (outer * 4 + m * 2 + core, k))
    lax.fori_loop(split, ncols, columns, 0)
    for i, m, k in mates(n_col, mid, col):
        await_bytes(mine, s_mate.at[i])
        await_bytes(mine, r_mate.at[i])
    half = biaso_ref.at[:, :, core]
    push(half, half, s_core, r_core, (outer * 4 + mid * 2 + 1 - core, col))
    await_bytes(half, s_core)
    await_bytes(half, r_core)
    for k, ref in ((0, xo_ref), (1, coto_ref)):
        def arrived(c, carry):
            await_bytes(ref.at[c, pl.ds(0, n_row - 1)], r_aa.at[k, c])
            return carry

        lax.fori_loop(0, ncols, arrived, 0)
        await_bytes(x_ref.at[pl.ds(0, n_row - 1)], s_aa.at[k])


def gather(x_tiles, cot_tiles, bias_tile):
    n_row, ncols, tile_rows, channels = x_tiles.shape
    n_col = lax.axis_size("col")
    n_out, n_mates = n_row // 4, 2 * n_col - 1
    cols = jax.ShapeDtypeStruct((ncols, n_row, tile_rows, channels), BF16)
    vmem = pl.BlockSpec(memory_space=VM)
    return pl.pallas_call(
        gather_kernel,
        in_specs=[vmem] * 3,
        out_specs=[vmem] * 3,
        out_shape=[cols, cols, jax.ShapeDtypeStruct((n_out, 2, 2, n_col) + bias_tile.shape, F32)],
        scratch_shapes=[
            DMA((2,)), DMA((2, ncols)), DMA((n_out - 1,)), DMA((n_out - 1,)),
            DMA((n_mates,)), DMA((n_mates,)), DMA, DMA, DMA((3,)),
        ],
        compiler_params=pltpu.CompilerParams(
            collective_id=0, has_side_effects=True, vmem_limit_bytes=40 * 1024 * 1024
        ),
    )(x_tiles, cot_tiles, bias_tile)


def scatter_kernel(
    att_ref, dn_ref, tot_ref, parts_ref, atto_ref, dno_ref, dbias_ref, sums_ref,
    rbuf, psend, prbuf, zsend, zrecv, qr, qs, qp, qz, qzs,
    s_aa, r_aa, s_out, r_out, s_mate, r_mate, s_core, r_core, s_ag, r_ag, s_agc, r_agc, s_loc,
):
    row, col, outer, mid, core = place()
    ncols, n_row = att_ref.shape[:2]
    n_out, n_col = tot_ref.shape[0], tot_ref.shape[3]
    other = (outer * 4 + mid * 2 + 1 - core, col)
    meet_all()
    core_moves = [(tot_ref.at[:, :, 1 - core], rbuf), (parts_ref.at[1 - core], qr)]
    for i, (src, dst) in enumerate(core_moves):
        push(src, dst, s_core.at[i], r_core.at[i], other)
    local = [
        pltpu.make_async_copy(att_ref.at[:, row], atto_ref.at[row], s_loc.at[0]),
        pltpu.make_async_copy(dn_ref.at[:, row], dno_ref.at[row], s_loc.at[1]),
    ]
    for copy in local:
        copy.start()

    def columns(c, carry):
        def peer(i, carry):
            r = lax.rem(row + i, n_row)
            push(att_ref.at[c, r], atto_ref.at[row, c], s_aa.at[0], r_aa.at[0], (r, col))
            push(dn_ref.at[c, r], dno_ref.at[row, c], s_aa.at[1], r_aa.at[1], (r, col))
            return carry

        return lax.fori_loop(1, n_row, peer, carry)

    split = ncols // 3
    lax.fori_loop(0, split, columns, 0)
    for i, (src, dst) in enumerate(core_moves):
        await_bytes(dst, s_core.at[i])
        await_bytes(dst, r_core.at[i])
    for m in range(2):
        for k in range(n_col):
            psend[m, k] = (tot_ref[:, m, core, k] + rbuf[:, m, k]).astype(BF16)
    qs[...] = parts_ref[core] + qr[...]
    for i, m, k in mates(n_col, mid, col):
        push(psend.at[m, k], prbuf.at[i], s_mate.at[0, i], r_mate.at[0, i], (outer * 4 + m * 2 + core, k))
        push(qs.at[m, k], qp.at[i], s_mate.at[1, i], r_mate.at[1, i], (outer * 4 + m * 2 + core, k))
    lax.fori_loop(split, 2 * split, columns, 0)
    for i, m, k in mates(n_col, mid, col):
        for j, ref in ((0, prbuf.at[i]), (1, qp.at[i])):
            await_bytes(ref, s_mate.at[j, i])
            await_bytes(ref, r_mate.at[j, i])
    own = psend[mid, col].astype(F32)
    mine = qs[mid, col]
    for i in range(2 * n_col - 1):
        own += prbuf[i].astype(F32)
        mine += qp[i]
    zsend[...] = own
    qzs[...] = mine
    for i in range(1, n_out):
        o = lax.rem(outer + i, n_out)
        there = (o * 4 + mid * 2 + core, col)
        push(zsend.at[o], zrecv.at[i - 1], s_out.at[0, i - 1], r_out.at[0, i - 1], there)
        push(qzs, qz.at[i - 1], s_out.at[1, i - 1], r_out.at[1, i - 1], there)
    lax.fori_loop(2 * split, ncols, columns, 0)
    for i in range(n_out - 1):
        for j, ref in ((0, zrecv.at[i]), (1, qz.at[i])):
            await_bytes(ref, s_out.at[j, i])
            await_bytes(ref, r_out.at[j, i])
    total, sums = zsend[outer], qzs[...]
    for i in range(n_out - 1):
        total += zrecv[i]
        sums += qz[i]
    dbias_ref[...] = total
    sums_ref[core, mid, col] = sums
    slab = sums_ref.at[core, mid, col]
    for i, m, k in mates(n_col, mid, col):
        push(slab, slab, s_ag.at[i], r_ag.at[i], (outer * 4 + m * 2 + core, k))
    for i in range(2 * n_col - 1):
        await_bytes(slab, s_ag.at[i])
        await_bytes(slab, r_ag.at[i])
    half = sums_ref.at[core]
    push(half, half, s_agc, r_agc, other)
    await_bytes(half, s_agc)
    await_bytes(half, r_agc)
    for copy in local:
        copy.wait()
    for k, ref in ((0, atto_ref), (1, dno_ref)):
        await_bytes(ref.at[pl.ds(0, n_row - 1)], s_aa.at[k])
        await_bytes(ref.at[pl.ds(0, n_row - 1)], r_aa.at[k])


def scatter(att_cols, dn_cols, total, parts):
    ncols, n_row, tile_rows, channels = att_cols.shape
    n_out, _, _, n_col = total.shape[:4]
    tile = total.shape[4:]
    n_mates, slab = 2 * n_col - 1, parts.shape[3:]
    tiles = jax.ShapeDtypeStruct((n_row, ncols, tile_rows, channels), BF16)
    vmem = pl.BlockSpec(memory_space=VM)
    return pl.pallas_call(
        scatter_kernel,
        in_specs=[vmem] * 4,
        out_specs=[vmem] * 4,
        out_shape=[
            tiles, tiles, jax.ShapeDtypeStruct(tile, F32), jax.ShapeDtypeStruct(parts.shape, F32)
        ],
        scratch_shapes=[
            VM((n_out, 2, n_col) + tile, F32),
            VM((2, n_col, n_out) + tile, BF16),
            VM((n_mates, n_out) + tile, BF16),
            VM((n_out,) + tile, F32),
            VM((n_out - 1,) + tile, F32),
            VM((2, n_col) + slab, F32),
            VM((2, n_col) + slab, F32),
            VM((n_mates,) + slab, F32),
            VM((n_out - 1,) + slab, F32),
            VM(slab, F32),
            DMA((2,)), DMA((2,)), DMA((2, n_out - 1)), DMA((2, n_out - 1)),
            DMA((2, n_mates)), DMA((2, n_mates)), DMA((2,)), DMA((2,)),
            DMA((n_mates,)), DMA((n_mates,)), DMA, DMA, DMA((2,)),
        ],
        compiler_params=pltpu.CompilerParams(
            collective_id=1, has_side_effects=True, vmem_limit_bytes=48 * 1024 * 1024
        ),
    )(att_cols, dn_cols, total, parts)


def share_kernel(mine_ref, sum_ref, got, send, recv):
    row, col = lax.axis_index("row"), lax.axis_index("col")
    n_row, n_col = lax.axis_size("row"), lax.axis_size("col")
    n_all = n_row * n_col
    meet_all()

    def one(i, carry):
        there = (lax.rem(row + i // n_col, n_row), lax.rem(col + lax.rem(i, n_col), n_col))
        push(mine_ref, got.at[i - 1], send, recv, there)
        return carry

    lax.fori_loop(1, n_all, one, 0)
    await_bytes(got, send)
    await_bytes(got, recv)
    sum_ref[...] = mine_ref[...] + jnp.sum(got[...], axis=0)


def share(mine):
    n_all = lax.axis_size("row") * lax.axis_size("col")
    vmem = pl.BlockSpec(memory_space=VM)
    return pl.pallas_call(
        share_kernel,
        in_specs=[vmem],
        out_specs=vmem,
        out_shape=jax.ShapeDtypeStruct(mine.shape, F32),
        scratch_shapes=[VM((n_all - 1,) + mine.shape, F32), DMA, DMA],
        compiler_params=pltpu.CompilerParams(collective_id=2, has_side_effects=True),
    )(mine)


def shards(pair, gain, projections, bias_weight, valid_len, out_cotangent):
    n_row = lax.axis_size("row")
    n_col = lax.axis_size("col")
    tile_rows, tile_cols, channels = pair.shape
    heads = bias_weight.shape[1]
    ncols = tile_cols // n_row
    pair_float = pair.astype(F32)
    average_value = jnp.mean(pair_float, axis=-1, keepdims=True)
    var = jnp.mean((pair_float - average_value) ** 2, axis=-1, keepdims=True)
    inverse_deviation = lax.rsqrt(var + EPS)
    centered_scaled = (pair_float - average_value) * inverse_deviation
    normalized_pair = (centered_scaled * gain).astype(BF16)
    bias_tile = jnp.einsum("abc,ch->hab", normalized_pair, bias_weight, preferred_element_type=F32)

    def to_columns(tile):
        return jnp.swapaxes(tile, 0, 1).reshape(n_row, ncols, tile_rows, channels)

    def to_tile(columns):
        return jnp.swapaxes(columns.reshape(tile_cols, tile_rows, channels), 0, 1)

    x_cols, cot_cols, bias = gather(to_columns(normalized_pair), to_columns(out_cotangent), bias_tile)
    w_in = jnp.swapaxes(projections[:4], 0, 1).reshape(channels, 4 * channels)
    att_cols, dn_cols, total, parts = attention(
        valid_len, x_cols, cot_cols, w_in, projections[4],
        bias.reshape(n_row, n_col, heads, tile_rows, tile_cols),
    )
    parts = jnp.swapaxes(parts.reshape(channels, 5, channels), 0, 1)
    att_tile, dn_tile, total, sums = scatter(
        att_cols, dn_cols,
        total.reshape(n_row // 4, 2, 2, n_col, heads, tile_rows, tile_cols),
        parts.reshape(2, 2, n_col, 5 * channels // (4 * n_col), channels),
    )
    projection_grad = sums.reshape(5, channels, channels)
    d_bias = total.astype(BF16)
    attended = to_tile(att_tile)
    bias_term = jnp.einsum("hab,ch->abc", d_bias, bias_weight, preferred_element_type=F32)
    bias_weight_part = jnp.einsum(
        "hab,abc->hc", d_bias, normalized_pair, preferred_element_type=F32
    )
    normalized_gradient = to_tile(dn_tile).astype(F32) + bias_term
    gain_partial_sum = jnp.sum(normalized_gradient * centered_scaled, axis=(0, 1))
    small = share(
        jnp.concatenate(
            [bias_weight_part, gain_partial_sum[None], jnp.zeros((7 - heads % 8, channels), F32)], axis=0
        )
    )
    bias_weight_grad, gain_gradient = small[:heads].T, small[heads]
    scaled_output = normalized_gradient * gain
    pair_gradient = inverse_deviation * (
        scaled_output
        - jnp.mean(scaled_output, axis=-1, keepdims=True)
        - centered_scaled * jnp.mean(scaled_output * centered_scaled, axis=-1, keepdims=True)
    )
    return (attended, pair_gradient, projection_grad, bias_weight_grad, gain_gradient)


def solution(mesh):
    placed = (P("row", "col", None), P(), P(), P(), P(), P("row", "col", None))
    return jax.shard_map(
        shards,
        mesh=mesh,
        in_specs=placed,
        out_specs=(P("row", "col", None), P("row", "col", None), P(), P(), P()),
        check_vma=False,
    )
```

```python
import functools

import jax
import jax.numpy as jnp
from jax import lax
from jax.experimental import pallas as pl
from jax.experimental.pallas import tpu as pltpu
from jax.sharding import PartitionSpec as P

EPS = 1e-05
F32 = jnp.float32
BF16 = jnp.bfloat16


def mm(left, right):
    return lax.dot_general(left, right, (((1,), (0,)), ((), ())), preferred_element_type=F32)


def mm_nt(left, right):
    return lax.dot_general(left, right, (((1,), (1,)), ((), ())), preferred_element_type=F32)


MESH = pl.DeviceIdType.MESH
VM = pltpu.VMEM
DMA = pltpu.SemaphoreType.DMA


def place():
    row, col = lax.axis_index("row"), lax.axis_index("col")
    return row, col, row // 4, lax.rem(row // 2, 2), lax.rem(row, 2)


def meet_all():
    row, col = lax.axis_index("row"), lax.axis_index("col")
    n_row, n_col = lax.axis_size("row"), lax.axis_size("col")
    barrier = pltpu.get_barrier_semaphore()

    def greet(i, carry):
        there = (lax.rem(row + i // n_col, n_row), lax.rem(col + lax.rem(i, n_col), n_col))
        pl.semaphore_signal(barrier, inc=1, device_id=there, device_id_type=MESH)
        return carry

    lax.fori_loop(1, n_row * n_col, greet, 0)
    pl.semaphore_wait(barrier, n_row * n_col - 1)


def push(src, dst, send, recv, where):
    pltpu.make_async_remote_copy(
        src_ref=src, dst_ref=dst, send_sem=send, recv_sem=recv,
        device_id=where, device_id_type=MESH,
    ).start()


def await_bytes(ref, sem):
    pltpu.make_async_copy(ref, ref, sem).wait()


def mates(n_col, mid, col):
    for i in range(1, 2 * n_col):
        yield i - 1, lax.rem(mid + i // n_col, 2), lax.rem(col + i % n_col, n_col)


def attend(heads, valid_ref, x_ref, cot_ref, w_in_ref, w_out_ref, bias_s, dbias_s, parts_ref, att_ref, dn_ref):
    n_row, tile_rows, channels = x_ref.shape
    rows = n_row * tile_rows
    width = channels // heads
    scale = width ** (-0.5)
    keep_lanes = lax.broadcasted_iota(jnp.int32, (rows, 1), 0) < valid_ref[0]
    x = x_ref[...].astype(F32).reshape(rows, channels).astype(BF16)
    cot = cot_ref[...].astype(F32).reshape(rows, channels).astype(BF16)
    proj = mm(x, w_in_ref[...])
    query = proj[:, :channels].astype(BF16)
    key_f = jnp.where(keep_lanes, proj[:, channels : 2 * channels], 0.0)
    key = key_f.astype(BF16)
    value_f = proj[:, 2 * channels : 3 * channels]
    value = value_f.astype(BF16)
    gate = jax.nn.sigmoid(proj[:, 3 * channels :])
    d_gated = mm_nt(cot, w_out_ref[...])
    d_context_f = d_gated * gate
    d_context = d_context_f.astype(BF16)
    key_t = jnp.transpose(key_f).astype(BF16)
    value_t = jnp.transpose(value_f).astype(BF16)
    lane_head = lax.broadcasted_iota(jnp.int32, (rows, channels), 1) // width
    ctx_parts, dq_parts = [], []
    dk = jnp.zeros((rows, channels), F32)
    dv = jnp.zeros((rows, channels), F32)
    for h in range(heads):
        mine = lane_head == h
        q_h = jnp.where(mine, query, jnp.zeros_like(query))
        dc_h = jnp.where(mine, d_context, jnp.zeros_like(d_context))
        s = mm_nt(key, q_h) * scale + bias_s[h]
        e = jnp.exp(s - jnp.max(s, axis=0, keepdims=True))
        p = e * (1.0 / jnp.sum(e, axis=0, keepdims=True))
        d_p = mm_nt(value, dc_h)
        delta = jnp.sum(p * d_p, axis=0, keepdims=True)
        ds = p * (d_p - delta)
        dbias_s[h] += ds
        p_b = p.astype(BF16)
        ds_b = ds.astype(BF16)
        ctx_parts.append(mm(value_t[h * width : (h + 1) * width], p_b))
        dq_parts.append(mm(key_t[h * width : (h + 1) * width], ds_b))
        dv += mm(p_b, dc_h)
        dk += mm(ds_b, q_h)
    context = jnp.transpose(jnp.concatenate(ctx_parts, axis=0)).astype(BF16).astype(F32)
    dq = (jnp.transpose(jnp.concatenate(dq_parts, axis=0)) * scale).astype(BF16)
    dk = (dk * scale).astype(BF16)
    dv = dv.astype(BF16)
    gated_f = gate * context
    gated = gated_f.astype(BF16)
    att = mm(gated, w_out_ref[...])
    att_ref[...] = att.reshape(n_row, tile_rows, channels).astype(att_ref.dtype)
    d_gate = (d_gated * context * gate * (1.0 - gate)).astype(BF16)
    grads = jnp.concatenate([dq, dk, dv, d_gate], axis=1)
    dn = mm_nt(grads, w_in_ref[...])
    dn_ref[...] = dn.reshape(n_row, tile_rows, channels).astype(dn_ref.dtype)
    x_t = jnp.transpose(x.astype(F32)).astype(BF16)
    parts_ref[:, : 4 * channels] += mm(x_t, grads)
    gated_t = jnp.transpose(gated.astype(F32)).astype(BF16)
    parts_ref[:, 4 * channels :] += mm(gated_t, cot)


def layer_kernel(
    heads, valid_ref, x_ref, cot_ref, bias_ref, w_in_ref, w_out_ref,
    atto_ref, dno_ref, dbias_ref, sums_ref,
    xc, cc, ball, bias_s, dbias_s, parts_s, att_s, dn_s,
    rbuf, psend, prbuf, zsend, zrecv, parts_c, qr, qs, qp, qz, qzs,
    s_fw, r_fw, s_bw, r_bw, s_bo, r_bo, s_bm, r_bm, s_bc, r_bc,
    s_out, r_out, s_mate, r_mate, s_core, r_core, s_ag, r_ag, s_agc, r_agc, s_loc,
):
    row, col, outer, mid, core = place()
    n_row, ncols, tile_rows, channels = x_ref.shape
    n_out, n_col = ball.shape[0], ball.shape[3]
    tile_cols = bias_ref.shape[2]
    rows = n_row * tile_rows
    other = (outer * 4 + mid * 2 + 1 - core, col)
    meet_all()
    for i in range(1, n_out):
        there = lax.rem(outer + i, n_out) * 4 + mid * 2 + core
        push(bias_ref, ball.at[outer, mid, core, col], s_bo.at[i - 1], r_bo.at[i - 1], (there, col))
    local = [
        pltpu.make_async_copy(bias_ref, ball.at[outer, mid, core, col], s_loc.at[0]),
        pltpu.make_async_copy(x_ref.at[row], xc.at[:, row], s_loc.at[1]),
        pltpu.make_async_copy(cot_ref.at[row], cc.at[:, row], s_loc.at[2]),
    ]
    for copy in local:
        copy.start()

    def send_out(c, carry):
        def peer(i, carry):
            r = lax.rem(row + i, n_row)
            push(x_ref.at[r, c], xc.at[c, row], s_fw.at[0], r_fw.at[0, c], (r, col))
            push(cot_ref.at[r, c], cc.at[c, row], s_fw.at[1], r_fw.at[1, c], (r, col))
            return carry

        return lax.fori_loop(1, n_row, peer, carry)

    def send_back(c, carry):
        def peer(i, carry):
            r = lax.rem(row + i, n_row)
            push(att_s.at[c, r], atto_ref.at[row, c], s_bw.at[0], r_bw.at[0], (r, col))
            push(dn_s.at[c, r], dno_ref.at[row, c], s_bw.at[1], r_bw.at[1], (r, col))
            return carry

        return lax.fori_loop(1, n_row, peer, carry)

    early = (ncols + 3) // 4
    lax.fori_loop(0, early, send_out, 0)
    dbias_s[...] = jnp.zeros_like(dbias_s)
    parts_s[...] = jnp.zeros_like(parts_s)
    for copy in local:
        copy.wait()
    for i in range(1, n_out):
        await_bytes(bias_ref, s_bo.at[i - 1])
        await_bytes(bias_ref, r_bo.at[i - 1])
    mine = ball.at[:, mid, core, col]
    for i, m, k in mates(n_col, mid, col):
        push(mine, mine, s_bm.at[i], r_bm.at[i], (outer * 4 + m * 2 + core, k))
    lax.fori_loop(early, ncols, send_out, 0)
    for i in range(2 * n_col - 1):
        await_bytes(mine, s_bm.at[i])
        await_bytes(mine, r_bm.at[i])
    half = ball.at[:, :, core]
    push(half, half, s_bc, r_bc, other)
    await_bytes(half, s_bc)
    await_bytes(half, r_bc)
    keep_lanes = lax.broadcasted_iota(jnp.int32, (rows, 1), 0) < valid_ref[0]
    for h in range(heads):
        for k in range(n_col):
            block = ball[:, :, :, k, h].reshape(rows, tile_cols)
            bias_s[h, :, k * tile_cols : (k + 1) * tile_cols] = jnp.where(keep_lanes, block, -1000000000.0)

    held = ncols * 5 // 12

    def column(c, carry):
        await_bytes(xc.at[c, pl.ds(0, n_row - 1)], r_fw.at[0, c])
        await_bytes(cc.at[c, pl.ds(0, n_row - 1)], r_fw.at[1, c])

        @pl.when((c > 0) & (c <= ncols - held))
        def _():
            send_back(c - 1, 0)

        attend(
            heads, valid_ref, xc.at[c], cc.at[c], w_in_ref, w_out_ref,
            bias_s, dbias_s, parts_s, att_s.at[c], dn_s.at[c],
        )
        return carry

    lax.fori_loop(0, ncols, column, 0)

    for h in range(heads):
        for k in range(n_col):
            block = dbias_s[h, :, k * tile_cols : (k + 1) * tile_cols]
            ball[:, :, :, k, h] = block.reshape(n_out, 2, 2, tile_rows, tile_cols)
    slab = parts_c.shape[3]
    for j in range(5 * channels // slab):
        lo = j * slab
        if channels % slab == 0:
            piece = parts_s[lo % channels : lo % channels + slab, lo // channels * channels : (lo // channels + 1) * channels]
        else:
            first = min(slab, channels - lo % channels)
            m = lo // channels
            piece = parts_s[lo % channels : lo % channels + first, m * channels : (m + 1) * channels]
            if first < slab:
                piece = jnp.concatenate([piece, parts_s[: slab - first, (m + 1) * channels : (m + 2) * channels]], axis=0)
        parts_c[j // (2 * n_col), j // n_col % 2, j % n_col] = piece
    core_moves = [(ball.at[:, :, 1 - core], rbuf), (parts_c.at[1 - core], qr)]
    for i, (src, dst) in enumerate(core_moves):
        push(src, dst, s_core.at[i], r_core.at[i], other)
    local = [
        pltpu.make_async_copy(att_s.at[:, row], atto_ref.at[row], s_loc.at[0]),
        pltpu.make_async_copy(dn_s.at[:, row], dno_ref.at[row], s_loc.at[1]),
    ]
    for copy in local:
        copy.start()
    for i, (src, dst) in enumerate(core_moves):
        await_bytes(dst, s_core.at[i])
        await_bytes(dst, r_core.at[i])
    for m in range(2):
        for k in range(n_col):
            psend[m, k] = (ball[:, m, core, k] + rbuf[:, m, k]).astype(BF16)
    qs[...] = parts_c[core] + qr[...]
    for i, m, k in mates(n_col, mid, col):
        push(psend.at[m, k], prbuf.at[i], s_mate.at[0, i], r_mate.at[0, i], (outer * 4 + m * 2 + core, k))
        push(qs.at[m, k], qp.at[i], s_mate.at[1, i], r_mate.at[1, i], (outer * 4 + m * 2 + core, k))
    for i in range(2 * n_col - 1):
        for j, ref in ((0, prbuf.at[i]), (1, qp.at[i])):
            await_bytes(ref, s_mate.at[j, i])
            await_bytes(ref, r_mate.at[j, i])
    own = psend[mid, col].astype(F32)
    mine = qs[mid, col]
    for i in range(2 * n_col - 1):
        own += prbuf[i].astype(F32)
        mine += qp[i]
    zsend[...] = own
    qzs[...] = mine
    for i in range(1, n_out):
        o = lax.rem(outer + i, n_out)
        there = (o * 4 + mid * 2 + core, col)
        push(zsend.at[o], zrecv.at[i - 1], s_out.at[0, i - 1], r_out.at[0, i - 1], there)
        push(qzs, qz.at[i - 1], s_out.at[1, i - 1], r_out.at[1, i - 1], there)
    lax.fori_loop(ncols - held, ncols, send_back, 0)
    for i in range(n_out - 1):
        for j, ref in ((0, zrecv.at[i]), (1, qz.at[i])):
            await_bytes(ref, s_out.at[j, i])
            await_bytes(ref, r_out.at[j, i])
    total, sums = zsend[outer], qzs[...]
    for i in range(n_out - 1):
        total += zrecv[i]
        sums += qz[i]
    dbias_ref[...] = total
    sums_ref[core, mid, col] = sums
    slab = sums_ref.at[core, mid, col]
    for i, m, k in mates(n_col, mid, col):
        push(slab, slab, s_ag.at[i], r_ag.at[i], (outer * 4 + m * 2 + core, k))
    for i in range(2 * n_col - 1):
        await_bytes(slab, s_ag.at[i])
        await_bytes(slab, r_ag.at[i])
    half = sums_ref.at[core]
    push(half, half, s_agc, r_agc, other)
    await_bytes(half, s_agc)
    await_bytes(half, r_agc)
    for copy in local:
        copy.wait()
    for k, ref in ((0, atto_ref), (1, dno_ref)):
        await_bytes(x_ref.at[pl.ds(0, n_row - 1)], s_fw.at[k])
        await_bytes(ref.at[pl.ds(0, n_row - 1)], s_bw.at[k])
        await_bytes(ref.at[pl.ds(0, n_row - 1)], r_bw.at[k])


def layer(valid_len, x_tiles, cot_tiles, bias_tile, w_in, w_out):
    n_row, ncols, tile_rows, channels = x_tiles.shape
    n_col = lax.axis_size("col")
    heads, _, tile_cols = tile = bias_tile.shape
    n_out, n_mates, rows = n_row // 4, 2 * n_col - 1, n_row * tile_rows
    slab = (5 * channels // (4 * n_col), channels)
    tiles = jax.ShapeDtypeStruct(x_tiles.shape, BF16)
    vmem = pl.BlockSpec(memory_space=VM)
    cols = VM((ncols, n_row, tile_rows, channels), BF16)
    return pl.pallas_call(
        functools.partial(layer_kernel, heads),
        in_specs=[pl.BlockSpec(memory_space=pltpu.SMEM)] + [vmem] * 5,
        out_specs=[vmem] * 4,
        out_shape=[
            tiles, tiles, jax.ShapeDtypeStruct(tile, F32),
            jax.ShapeDtypeStruct((2, 2, n_col) + slab, F32),
        ],
        scratch_shapes=[
            cols, cols,
            VM((n_out, 2, 2, n_col) + tile, F32),
            VM((heads, rows, rows), F32),
            VM((heads, rows, rows), F32),
            VM((channels, 5 * channels), F32),
            cols, cols,
            VM((n_out, 2, n_col) + tile, F32),
            VM((2, n_col, n_out) + tile, BF16),
            VM((n_mates, n_out) + tile, BF16),
            VM((n_out,) + tile, F32),
            VM((n_out - 1,) + tile, F32),
            VM((2, 2, n_col) + slab, F32),
            VM((2, n_col) + slab, F32),
            VM((2, n_col) + slab, F32),
            VM((n_mates,) + slab, F32),
            VM((n_out - 1,) + slab, F32),
            VM(slab, F32),
            DMA((2,)), DMA((2, ncols)), DMA((2,)), DMA((2,)),
            DMA((n_out - 1,)), DMA((n_out - 1,)), DMA((n_mates,)), DMA((n_mates,)), DMA, DMA,
            DMA((2, n_out - 1)), DMA((2, n_out - 1)),
            DMA((2, n_mates)), DMA((2, n_mates)), DMA((2,)), DMA((2,)),
            DMA((n_mates,)), DMA((n_mates,)), DMA, DMA, DMA((3,)),
        ],
        compiler_params=pltpu.CompilerParams(
            collective_id=0, has_side_effects=True, vmem_limit_bytes=60 * 1024 * 1024
        ),
    )(valid_len, x_tiles, cot_tiles, bias_tile, w_in, w_out)


def share_kernel(mine_ref, sum_ref, got, send, recv):
    row, col = lax.axis_index("row"), lax.axis_index("col")
    n_row, n_col = lax.axis_size("row"), lax.axis_size("col")
    n_all = n_row * n_col
    meet_all()

    def one(i, carry):
        there = (lax.rem(row + i // n_col, n_row), lax.rem(col + lax.rem(i, n_col), n_col))
        push(mine_ref, got.at[i - 1], send, recv, there)
        return carry

    lax.fori_loop(1, n_all, one, 0)
    await_bytes(got, send)
    await_bytes(got, recv)
    sum_ref[...] = mine_ref[...] + jnp.sum(got[...], axis=0)


def share(mine):
    n_all = lax.axis_size("row") * lax.axis_size("col")
    vmem = pl.BlockSpec(memory_space=VM)
    return pl.pallas_call(
        share_kernel,
        in_specs=[vmem],
        out_specs=vmem,
        out_shape=jax.ShapeDtypeStruct(mine.shape, F32),
        scratch_shapes=[VM((n_all - 1,) + mine.shape, F32), DMA, DMA],
        compiler_params=pltpu.CompilerParams(collective_id=1, has_side_effects=True),
    )(mine)


def shards(pair, gain, projections, bias_weight, valid_len, out_cotangent):
    n_row = lax.axis_size("row")
    n_col = lax.axis_size("col")
    tile_rows, tile_cols, channels = pair.shape
    heads = bias_weight.shape[1]
    ncols = tile_cols // n_row
    pair_float = pair.astype(F32)
    average_value = jnp.mean(pair_float, axis=-1, keepdims=True)
    var = jnp.mean((pair_float - average_value) ** 2, axis=-1, keepdims=True)
    inverse_deviation = lax.rsqrt(var + EPS)
    centered_scaled = (pair_float - average_value) * inverse_deviation
    normalized_pair = (centered_scaled * gain).astype(BF16)
    bias_tile = jnp.einsum("abc,ch->hab", normalized_pair, bias_weight, preferred_element_type=F32)

    def to_columns(tile):
        return jnp.swapaxes(tile, 0, 1).reshape(n_row, ncols, tile_rows, channels)

    def to_tile(columns):
        return jnp.swapaxes(columns.reshape(tile_cols, tile_rows, channels), 0, 1)

    w_in = jnp.swapaxes(projections[:4], 0, 1).reshape(channels, 4 * channels)
    att_tile, dn_tile, total, sums = layer(
        valid_len, to_columns(normalized_pair), to_columns(out_cotangent), bias_tile, w_in, projections[4]
    )
    projection_grad = sums.reshape(5, channels, channels)
    d_bias = total.astype(BF16)
    attended = to_tile(att_tile)
    bias_term = jnp.einsum("hab,ch->abc", d_bias, bias_weight, preferred_element_type=F32)
    bias_weight_part = jnp.einsum(
        "hab,abc->hc", d_bias, normalized_pair, preferred_element_type=F32
    )
    normalized_gradient = to_tile(dn_tile).astype(F32) + bias_term
    gain_partial_sum = jnp.sum(normalized_gradient * centered_scaled, axis=(0, 1))
    small = share(
        jnp.concatenate(
            [bias_weight_part, gain_partial_sum[None], jnp.zeros((7 - heads % 8, channels), F32)], axis=0
        )
    )
    bias_weight_grad, gain_gradient = small[:heads].T, small[heads]
    scaled_output = normalized_gradient * gain
    pair_gradient = inverse_deviation * (
        scaled_output
        - jnp.mean(scaled_output, axis=-1, keepdims=True)
        - centered_scaled * jnp.mean(scaled_output * centered_scaled, axis=-1, keepdims=True)
    )
    return (attended, pair_gradient, projection_grad, bias_weight_grad, gain_gradient)


def solution(mesh):
    placed = (P("row", "col", None), P(), P(), P(), P(), P("row", "col", None))
    return jax.shard_map(
        shards,
        mesh=mesh,
        in_specs=placed,
        out_specs=(P("row", "col", None), P("row", "col", None), P(), P(), P()),
        check_vma=False,
    )
```

```python
import functools

import jax
import jax.numpy as jnp
from jax import lax
from jax.experimental import pallas as pl
from jax.experimental.pallas import tpu as pltpu
from jax.sharding import PartitionSpec as P

EPS = 1e-05
F32 = jnp.float32
BF16 = jnp.bfloat16


def mm(left, right):
    return lax.dot_general(left, right, (((1,), (0,)), ((), ())), preferred_element_type=F32)


def mm_nt(left, right):
    return lax.dot_general(left, right, (((1,), (1,)), ((), ())), preferred_element_type=F32)


MESH = pl.DeviceIdType.MESH
VM = pltpu.VMEM
DMA = pltpu.SemaphoreType.DMA


def place():
    row, col = lax.axis_index("row"), lax.axis_index("col")
    return row, col, row // 4, lax.rem(row // 2, 2), lax.rem(row, 2)


def greet_all():
    row, col = lax.axis_index("row"), lax.axis_index("col")
    n_row, n_col = lax.axis_size("row"), lax.axis_size("col")
    barrier = pltpu.get_barrier_semaphore()

    def greet(i, carry):
        there = (lax.rem(row + i // n_col, n_row), lax.rem(col + lax.rem(i, n_col), n_col))
        pl.semaphore_signal(barrier, inc=1, device_id=there, device_id_type=MESH)
        return carry

    lax.fori_loop(1, n_row * n_col, greet, 0)
    return barrier, n_row * n_col - 1


def push(src, dst, send, recv, where):
    pltpu.make_async_remote_copy(
        src_ref=src, dst_ref=dst, send_sem=send, recv_sem=recv,
        device_id=where, device_id_type=MESH,
    ).start()


def await_bytes(ref, sem):
    pltpu.make_async_copy(ref, ref, sem).wait()


def mates(n_col, mid, col):
    for i in range(1, 2 * n_col):
        yield i - 1, lax.rem(mid + i // n_col, 2), lax.rem(col + i % n_col, n_col)


def norm(x_f):
    average = jnp.mean(x_f, axis=-1, keepdims=True)
    centered = x_f - average
    inverse = lax.rsqrt(jnp.mean(centered * centered, axis=-1, keepdims=True) + EPS)
    return centered * inverse, inverse


def fold_rows(x_f):
    return jnp.sum(x_f.reshape(-1, 8, x_f.shape[-1]), axis=0)


def attend(
    heads, valid_ref, x_ref, cot_ref, gain, w_in_ref, w_out_ref, bias_s, dbias_s, parts_ref, gain_s, att_ref, dn_ref
):
    n_row, tile_rows, channels = x_ref.shape
    rows = n_row * tile_rows
    width = channels // heads
    scale = width ** (-0.5)
    keep_lanes = lax.broadcasted_iota(jnp.int32, (rows, 1), 0) < valid_ref[0]
    x_hat, _ = norm(x_ref[...].astype(F32).reshape(rows, channels))
    x_f = x_hat * gain
    x = x_f.astype(BF16)
    cot = cot_ref[...].astype(F32).reshape(rows, channels).astype(BF16)
    proj = mm(x, w_in_ref[...])
    query = proj[:, :channels].astype(BF16)
    key_f = jnp.where(keep_lanes, proj[:, channels : 2 * channels], 0.0)
    key = key_f.astype(BF16)
    value_f = proj[:, 2 * channels : 3 * channels]
    value = value_f.astype(BF16)
    gate = jax.nn.sigmoid(proj[:, 3 * channels :])
    d_gated = mm_nt(cot, w_out_ref[...])
    d_context_f = d_gated * gate
    d_context = d_context_f.astype(BF16)
    key_t = jnp.transpose(key_f).astype(BF16)
    value_t = jnp.transpose(value_f).astype(BF16)
    lane_head = lax.broadcasted_iota(jnp.int32, (rows, channels), 1) // width
    ctx_parts, dq_parts = [], []
    dk = jnp.zeros((rows, channels), F32)
    dv = jnp.zeros((rows, channels), F32)
    for h in range(heads):
        mine = lane_head == h
        q_h = jnp.where(mine, query, jnp.zeros_like(query))
        dc_h = jnp.where(mine, d_context, jnp.zeros_like(d_context))
        s = mm_nt(key, q_h) * scale + bias_s[h]
        e = jnp.exp(s - jnp.max(s, axis=0, keepdims=True))
        p = e * (1.0 / jnp.sum(e, axis=0, keepdims=True))
        d_p = mm_nt(value, dc_h)
        delta = jnp.sum(p * d_p, axis=0, keepdims=True)
        ds = p * (d_p - delta)
        dbias_s[h] += ds
        p_b = p.astype(BF16)
        ds_b = ds.astype(BF16)
        ctx_parts.append(mm(value_t[h * width : (h + 1) * width], p_b))
        dq_parts.append(mm(key_t[h * width : (h + 1) * width], ds_b))
        dv += mm(p_b, dc_h)
        dk += mm(ds_b, q_h)
    context = jnp.transpose(jnp.concatenate(ctx_parts, axis=0)).astype(BF16).astype(F32)
    dq = (jnp.transpose(jnp.concatenate(dq_parts, axis=0)) * scale).astype(BF16)
    dk = (dk * scale).astype(BF16)
    dv = dv.astype(BF16)
    gated_f = gate * context
    gated = gated_f.astype(BF16)
    att = mm(gated, w_out_ref[...])
    att_ref[...] = att.reshape(n_row, tile_rows, channels).astype(att_ref.dtype)
    d_gate = (d_gated * context * gate * (1.0 - gate)).astype(BF16)
    grads = jnp.concatenate([dq, dk, dv, d_gate], axis=1)
    dn = mm_nt(grads, w_in_ref[...])
    dn_ref[...] = dn.reshape(n_row, tile_rows, channels).astype(dn_ref.dtype)
    gain_s[...] += fold_rows(dn * x_hat)
    x_t = jnp.transpose(x_f).astype(BF16)
    parts_ref[:, : 4 * channels] += mm(x_t, grads)
    gated_t = jnp.transpose(gated_f).astype(BF16)
    parts_ref[:, 4 * channels :] += mm(gated_t, cot)


def layer_kernel(
    heads, valid_ref, pair_ref, x_ref, cot_ref, gain_ref, bwt_ref, proj_ref,
    atto_ref, pgo_ref, sums_ref, small_ref,
    btile, x_hat_s, normed_s, w_in, xc, cc, ball, bias_s, dbias_s, parts_s, gain_s, att_s, dn_s, dno, bterm,
    rbuf, psend, prbuf, zsend, zrecv, parts_c, qr, qs, qp, qz, qzs, small_s, small_g,
    s_fw, r_fw, s_bw, r_bw, s_bo, r_bo, s_bm, r_bm, s_bc, r_bc,
    s_out, r_out, s_mate, r_mate, s_core, r_core, s_ag, r_ag, s_agc, r_agc, s_small, r_small, s_loc,
):
    row, col, outer, mid, core = place()
    n_row, ncols, tile_rows, channels = x_ref.shape
    n_out, n_col = ball.shape[0], ball.shape[3]
    tile_cols = pair_ref.shape[1]
    rows = n_row * tile_rows
    other = (outer * 4 + mid * 2 + 1 - core, col)
    w_out_ref = proj_ref.at[4]
    gain = gain_ref[...]
    barrier, n_others = greet_all()

    def lanes(h):
        return h // 2, slice(h % 2 * tile_cols, (h % 2 + 1) * tile_cols)

    for a in range(tile_rows):
        x_hat, _ = norm(pair_ref[a].astype(F32))
        normed = (x_hat * gain).astype(BF16)
        x_hat_s[a] = x_hat
        normed_s[a] = normed
        bias_a = mm_nt(bwt_ref[...], normed)
        for h in range(heads):
            p, where = lanes(h)
            btile[p, a : a + 1, where] = bias_a[h : h + 1]
    pl.semaphore_wait(barrier, n_others)
    for i in range(1, n_out):
        there = lax.rem(outer + i, n_out) * 4 + mid * 2 + core
        push(btile, ball.at[outer, mid, core, col], s_bo.at[i - 1], r_bo.at[i - 1], (there, col))
    local = [
        pltpu.make_async_copy(btile, ball.at[outer, mid, core, col], s_loc.at[0]),
        pltpu.make_async_copy(x_ref.at[row], xc.at[:, row], s_loc.at[1]),
        pltpu.make_async_copy(cot_ref.at[row], cc.at[:, row], s_loc.at[2]),
    ]
    for copy in local:
        copy.start()

    def send_out(c, carry):
        def peer(i, carry):
            r = lax.rem(row + i, n_row)
            push(x_ref.at[r, c], xc.at[c, row], s_fw.at[0], r_fw.at[0, c], (r, col))
            push(cot_ref.at[r, c], cc.at[c, row], s_fw.at[1], r_fw.at[1, c], (r, col))
            return carry

        return lax.fori_loop(1, n_row, peer, carry)

    def send_back(c, carry):
        def peer(i, carry):
            r = lax.rem(row + i, n_row)
            push(att_s.at[c, r], atto_ref.at[row, c], s_bw.at[0], r_bw.at[0, c], (r, col))
            push(dn_s.at[c, r], dno.at[c, row], s_bw.at[1], r_bw.at[1, c], (r, col))
            return carry

        return lax.fori_loop(1, n_row, peer, carry)

    early = (ncols + 3) // 4
    lax.fori_loop(0, early, send_out, 0)
    dbias_s[...] = jnp.zeros_like(dbias_s)
    parts_s[...] = jnp.zeros_like(parts_s)
    gain_s[...] = jnp.zeros_like(gain_s)
    for m in range(4):
        w_in[:, m * channels : (m + 1) * channels] = proj_ref[m]
    for copy in local:
        copy.wait()
    for i in range(1, n_out):
        await_bytes(btile, s_bo.at[i - 1])
        await_bytes(btile, r_bo.at[i - 1])
    mine = ball.at[:, mid, core, col]
    for i, m, k in mates(n_col, mid, col):
        push(mine, mine, s_bm.at[i], r_bm.at[i], (outer * 4 + m * 2 + core, k))
    lax.fori_loop(early, ncols, send_out, 0)
    for i in range(2 * n_col - 1):
        await_bytes(mine, s_bm.at[i])
        await_bytes(mine, r_bm.at[i])
    half = ball.at[:, :, core]
    push(half, half, s_bc, r_bc, other)
    await_bytes(half, s_bc)
    await_bytes(half, r_bc)
    keep_lanes = lax.broadcasted_iota(jnp.int32, (rows, 1), 0) < valid_ref[0]
    for h in range(heads):
        p, where = lanes(h)
        for k in range(n_col):
            block = ball[:, :, :, k, p].reshape(rows, 2 * tile_cols)[:, where]
            bias_s[h, :, k * tile_cols : (k + 1) * tile_cols] = jnp.where(keep_lanes, block, -1000000000.0)

    held = ncols * 5 // 12

    def column(c, carry):
        await_bytes(xc.at[c, pl.ds(0, n_row - 1)], r_fw.at[0, c])
        await_bytes(cc.at[c, pl.ds(0, n_row - 1)], r_fw.at[1, c])

        @pl.when((c > 0) & (c <= ncols - held))
        def _():
            send_back(c - 1, 0)

        attend(
            heads, valid_ref, xc.at[c], cc.at[c], gain, w_in, w_out_ref,
            bias_s, dbias_s, parts_s, gain_s, att_s.at[c], dn_s.at[c],
        )
        return carry

    lax.fori_loop(0, ncols, column, 0)

    for h in range(heads):
        p, where = lanes(h)
        for k in range(n_col):
            block = dbias_s[h, :, k * tile_cols : (k + 1) * tile_cols]
            ball[:, :, :, k, p, :, where] = block.reshape(n_out, 2, 2, tile_rows, tile_cols)
    slab = parts_c.shape[3]
    for j in range(5 * channels // slab):
        m, lo = j * slab // channels, j * slab % channels
        first = min(slab, channels - lo)
        piece = parts_s[lo : lo + first, m * channels : (m + 1) * channels]
        if first < slab:
            rest = parts_s[: slab - first, (m + 1) * channels : (m + 2) * channels]
            piece = jnp.concatenate([piece, rest], axis=0)
        parts_c[j // (2 * n_col), j // n_col % 2, j % n_col] = piece
    core_moves = [(ball.at[:, :, 1 - core], rbuf), (parts_c.at[1 - core], qr)]
    for i, (src, dst) in enumerate(core_moves):
        push(src, dst, s_core.at[i], r_core.at[i], other)
    local = [
        pltpu.make_async_copy(att_s.at[:, row], atto_ref.at[row], s_loc.at[0]),
        pltpu.make_async_copy(dn_s.at[:, row], dno.at[:, row], s_loc.at[1]),
    ]
    for copy in local:
        copy.start()
    for i, (src, dst) in enumerate(core_moves):
        await_bytes(dst, s_core.at[i])
        await_bytes(dst, r_core.at[i])
    for m in range(2):
        for k in range(n_col):
            psend[m, k] = (ball[:, m, core, k] + rbuf[:, m, k]).astype(BF16)
    qs[...] = parts_c[core] + qr[...]
    for i, m, k in mates(n_col, mid, col):
        push(psend.at[m, k], prbuf.at[i], s_mate.at[0, i], r_mate.at[0, i], (outer * 4 + m * 2 + core, k))
        push(qs.at[m, k], qp.at[i], s_mate.at[1, i], r_mate.at[1, i], (outer * 4 + m * 2 + core, k))
    for i in range(2 * n_col - 1):
        for j, ref in ((0, prbuf.at[i]), (1, qp.at[i])):
            await_bytes(ref, s_mate.at[j, i])
            await_bytes(ref, r_mate.at[j, i])
    own = psend[mid, col].astype(F32)
    mine = qs[mid, col]
    for i in range(2 * n_col - 1):
        own += prbuf[i].astype(F32)
        mine += qp[i]
    zsend[...] = own
    qzs[...] = mine
    for i in range(1, n_out):
        o = lax.rem(outer + i, n_out)
        there = (o * 4 + mid * 2 + core, col)
        push(zsend.at[o], zrecv.at[i - 1], s_out.at[0, i - 1], r_out.at[0, i - 1], there)
        push(qzs, qz.at[i - 1], s_out.at[1, i - 1], r_out.at[1, i - 1], there)
    last = (held + 1) // 2
    lax.fori_loop(ncols - held, ncols - last, send_back, 0)
    for i in range(n_out - 1):
        for j, ref in ((0, zrecv.at[i]), (1, qz.at[i])):
            await_bytes(ref, s_out.at[j, i])
            await_bytes(ref, r_out.at[j, i])
    total, sums = zsend[outer], qzs[...]
    for i in range(n_out - 1):
        total += zrecv[i]
        sums += qz[i]
    sums_ref[core, mid, col] = sums
    mine = sums_ref.at[core, mid, col]
    for i, m, k in mates(n_col, mid, col):
        push(mine, mine, s_ag.at[i], r_ag.at[i], (outer * 4 + m * 2 + core, k))

    btile[...] = total
    no_heads = jnp.zeros((8 - heads, tile_cols), F32)
    weight_part = jnp.zeros((8, channels), F32)
    gain_part = gain_s[...]
    for a in range(tile_rows):
        d_rows = [btile[p, a : a + 1, where] for p, where in map(lanes, range(heads))]
        d_a = jnp.concatenate(d_rows + [no_heads], axis=0).astype(BF16)
        term = lax.dot_general(d_a, bwt_ref[...], (((0,), (0,)), ((), ())), preferred_element_type=F32)
        bterm[pl.ds(a, tile_cols, stride=tile_rows), :] = term
        weight_part += mm(d_a, normed_s[a])
        gain_part += fold_rows(term * x_hat_s[a])
    at = lax.broadcasted_iota(jnp.int32, (8, channels), 0)
    gain_row = jnp.broadcast_to(jnp.sum(gain_part, axis=0, keepdims=True), (8, channels))
    small_s[...] = jnp.where(at < heads, weight_part, jnp.where(at == heads, gain_row, 0.0))

    def spread(i, carry):
        there = (lax.rem(row + i // n_col, n_row), lax.rem(col + lax.rem(i, n_col), n_col))
        push(small_s, small_g.at[i - 1], s_small, r_small, there)
        return carry

    lax.fori_loop(1, n_row * n_col, spread, 0)
    lax.fori_loop(ncols - last, ncols, send_back, 0)
    for copy in local:
        copy.wait()

    def finish(c, carry):
        await_bytes(dno.at[c, pl.ds(0, n_row - 1)], r_bw.at[1, c])
        x_hat, inverse = norm(x_ref[:, c].astype(F32).reshape(rows, channels))
        block = [bterm[pl.ds(pl.multiple_of((r * ncols + c) * tile_rows, 8), tile_rows), :] for r in range(n_row)]
        g = (dno[c].astype(F32).reshape(rows, channels) + jnp.concatenate(block, axis=0)) * gain
        inner = jnp.mean(g * x_hat, axis=-1, keepdims=True)
        out = inverse * (g - jnp.mean(g, axis=-1, keepdims=True) - x_hat * inner)
        pgo_ref[:, c] = out.reshape(n_row, tile_rows, channels)
        return carry

    early = ncols - last
    lax.fori_loop(0, early, finish, 0)
    for i in range(2 * n_col - 1):
        await_bytes(mine, s_ag.at[i])
        await_bytes(mine, r_ag.at[i])
    half = sums_ref.at[core]
    push(half, half, s_agc, r_agc, other)
    lax.fori_loop(early, ncols, finish, 0)
    await_bytes(half, s_agc)
    await_bytes(half, r_agc)
    await_bytes(small_g, s_small)
    await_bytes(small_g, r_small)
    small_ref[...] = small_s[...] + jnp.sum(small_g[...], axis=0)

    def came_back(c, carry):
        await_bytes(att_s.at[c, pl.ds(0, n_row - 1)], r_bw.at[0, c])
        return carry

    lax.fori_loop(0, ncols, came_back, 0)
    for k in range(2):
        await_bytes(x_ref.at[pl.ds(0, n_row - 1)], s_fw.at[k])
        await_bytes(x_ref.at[pl.ds(0, n_row - 1)], s_bw.at[k])


def layer(heads, valid_len, pair, x_tiles, cot_tiles, gain, bias_rows, projections):
    n_row, ncols, tile_rows, channels = x_tiles.shape
    n_col = lax.axis_size("col")
    tile_cols = pair.shape[1]
    tile = (heads // 2, tile_rows, 2 * tile_cols)
    n_out, n_mates, rows = n_row // 4, 2 * n_col - 1, n_row * tile_rows
    slab = (5 * channels // (4 * n_col), channels)
    vmem = pl.BlockSpec(memory_space=VM)
    cols = VM((ncols, n_row, tile_rows, channels), BF16)
    return pl.pallas_call(
        functools.partial(layer_kernel, heads),
        in_specs=[pl.BlockSpec(memory_space=pltpu.SMEM)] + [vmem] * 6,
        out_specs=[vmem] * 4,
        out_shape=[
            jax.ShapeDtypeStruct(x_tiles.shape, BF16),
            jax.ShapeDtypeStruct(x_tiles.shape, F32),
            jax.ShapeDtypeStruct((2, 2, n_col) + slab, F32),
            jax.ShapeDtypeStruct((8, channels), F32),
        ],
        scratch_shapes=[
            VM(tile, F32),
            VM(pair.shape, F32),
            VM(pair.shape, BF16),
            VM((channels, 4 * channels), BF16),
            cols, cols,
            VM((n_out, 2, 2, n_col) + tile, F32),
            VM((heads, rows, rows), F32),
            VM((heads, rows, rows), F32),
            VM((channels, 5 * channels), F32),
            VM((8, channels), F32),
            cols, cols, cols,
            VM((tile_cols * tile_rows, channels), F32),
            VM((n_out, 2, n_col) + tile, F32),
            VM((2, n_col, n_out) + tile, BF16),
            VM((n_mates, n_out) + tile, BF16),
            VM((n_out,) + tile, F32),
            VM((n_out - 1,) + tile, F32),
            VM((2, 2, n_col) + slab, F32),
            VM((2, n_col) + slab, F32),
            VM((2, n_col) + slab, F32),
            VM((n_mates,) + slab, F32),
            VM((n_out - 1,) + slab, F32),
            VM(slab, F32),
            VM((8, channels), F32),
            VM((n_row * n_col - 1, 8, channels), F32),
            DMA((2,)), DMA((2, ncols)), DMA((2,)), DMA((2, ncols)),
            DMA((n_out - 1,)), DMA((n_out - 1,)), DMA((n_mates,)), DMA((n_mates,)), DMA, DMA,
            DMA((2, n_out - 1)), DMA((2, n_out - 1)),
            DMA((2, n_mates)), DMA((2, n_mates)), DMA((2,)), DMA((2,)),
            DMA((n_mates,)), DMA((n_mates,)), DMA, DMA, DMA, DMA, DMA((3,)),
        ],
        compiler_params=pltpu.CompilerParams(
            collective_id=0, has_side_effects=True, vmem_limit_bytes=62 * 1024 * 1024
        ),
    )(valid_len, pair, x_tiles, cot_tiles, gain, bias_rows, projections)


def shards(pair, gain, projections, bias_weight, valid_len, out_cotangent):
    n_row = lax.axis_size("row")
    tile_rows, tile_cols, channels = pair.shape
    heads = bias_weight.shape[1]

    def to_columns(tile):
        return jnp.swapaxes(tile, 0, 1).reshape(n_row, tile_cols // n_row, tile_rows, channels)

    def to_tile(columns):
        return jnp.swapaxes(columns.reshape(tile_cols, tile_rows, channels), 0, 1)

    bias_rows = jnp.pad(bias_weight.T, ((0, 8 - heads), (0, 0)))
    attended, pair_gradient, sums, small = layer(
        heads, valid_len, pair, to_columns(pair), to_columns(out_cotangent), gain[None], bias_rows, projections
    )
    return (
        to_tile(attended),
        to_tile(pair_gradient),
        sums.reshape(5, channels, channels),
        small[:heads].T,
        small[heads],
    )


def solution(mesh):
    placed = (P("row", "col", None), P(), P(), P(), P(), P("row", "col", None))
    return jax.shard_map(
        shards,
        mesh=mesh,
        in_specs=placed,
        out_specs=(P("row", "col", None), P("row", "col", None), P(), P(), P()),
        check_vma=False,
    )
```

```python
import functools

import jax
import jax.numpy as jnp
from jax import lax
from jax.experimental import pallas as pl
from jax.experimental.pallas import tpu as pltpu
from jax.sharding import PartitionSpec as P

EPS = 1e-05
F32 = jnp.float32
BF16 = jnp.bfloat16


def mm(left, right):
    return lax.dot_general(left, right, (((1,), (0,)), ((), ())), preferred_element_type=F32)


def mm_nt(left, right):
    return lax.dot_general(left, right, (((1,), (1,)), ((), ())), preferred_element_type=F32)


MESH = pl.DeviceIdType.MESH
VM = pltpu.VMEM
DMA = pltpu.SemaphoreType.DMA


def place():
    row, col = lax.axis_index("row"), lax.axis_index("col")
    return row, col, row // 4, lax.rem(row // 2, 2), lax.rem(row, 2)


def greet_all():
    row, col = lax.axis_index("row"), lax.axis_index("col")
    n_row, n_col = lax.axis_size("row"), lax.axis_size("col")
    barrier = pltpu.get_barrier_semaphore()

    def greet(i, carry):
        there = (lax.rem(row + i // n_col, n_row), lax.rem(col + lax.rem(i, n_col), n_col))
        pl.semaphore_signal(barrier, inc=1, device_id=there, device_id_type=MESH)
        return carry

    lax.fori_loop(1, n_row * n_col, greet, 0)
    return barrier, n_row * n_col - 1


def push(src, dst, send, recv, where):
    pltpu.make_async_remote_copy(
        src_ref=src, dst_ref=dst, send_sem=send, recv_sem=recv,
        device_id=where, device_id_type=MESH,
    ).start()


def await_bytes(ref, sem):
    pltpu.make_async_copy(ref, ref, sem).wait()


def mates(n_col, mid, col):
    for i in range(1, 2 * n_col):
        yield i - 1, lax.rem(mid + i // n_col, 2), lax.rem(col + i % n_col, n_col)


def norm(x_f):
    average = jnp.mean(x_f, axis=-1, keepdims=True)
    centered = x_f - average
    inverse = lax.rsqrt(jnp.mean(centered * centered, axis=-1, keepdims=True) + EPS)
    return centered * inverse, inverse


def fold_rows(x_f):
    return jnp.sum(x_f.reshape(-1, 8, x_f.shape[-1]), axis=0)


def attend(
    heads, valid_ref, x_ref, cot_ref, gain, w_in_ref, w_out_ref, bias_s, dbias_s, parts_ref, gain_s, att_ref, dn_ref
):
    n_row, tile_rows, channels = x_ref.shape
    rows = n_row * tile_rows
    width = channels // heads
    scale = width ** (-0.5)
    keep_lanes = lax.broadcasted_iota(jnp.int32, (rows, 1), 0) < valid_ref[0]
    x_hat, _ = norm(x_ref[...].astype(F32).reshape(rows, channels))
    x_f = x_hat * gain
    x = x_f.astype(BF16)
    cot = cot_ref[...].astype(F32).reshape(rows, channels).astype(BF16)
    proj = mm(x, w_in_ref[...])
    query = proj[:, :channels].astype(BF16)
    key_f = jnp.where(keep_lanes, proj[:, channels : 2 * channels], 0.0)
    key = key_f.astype(BF16)
    value_f = proj[:, 2 * channels : 3 * channels]
    value = value_f.astype(BF16)
    gate = jax.nn.sigmoid(proj[:, 3 * channels :])
    d_gated = mm_nt(cot, w_out_ref[...])
    d_context_f = d_gated * gate
    d_context = d_context_f.astype(BF16)
    key_t = jnp.transpose(key_f).astype(BF16)
    value_t = jnp.transpose(value_f).astype(BF16)
    lane_head = lax.broadcasted_iota(jnp.int32, (rows, channels), 1) // width
    ctx_parts, dq_parts = [], []
    dk = jnp.zeros((rows, channels), F32)
    dv = jnp.zeros((rows, channels), F32)
    for h in range(heads):
        mine = lane_head == h
        q_h = jnp.where(mine, query, jnp.zeros_like(query))
        dc_h = jnp.where(mine, d_context, jnp.zeros_like(d_context))
        s = mm_nt(key, q_h) * scale + bias_s[h]
        e = jnp.exp(s - jnp.max(s, axis=0, keepdims=True))
        p = e * (1.0 / jnp.sum(e, axis=0, keepdims=True))
        d_p = mm_nt(value, dc_h)
        delta = jnp.sum(p * d_p, axis=0, keepdims=True)
        ds = p * (d_p - delta)
        dbias_s[h] += ds
        p_b = p.astype(BF16)
        ds_b = ds.astype(BF16)
        ctx_parts.append(mm(value_t[h * width : (h + 1) * width], p_b))
        dq_parts.append(mm(key_t[h * width : (h + 1) * width], ds_b))
        dv += mm(p_b, dc_h)
        dk += mm(ds_b, q_h)
    context = jnp.transpose(jnp.concatenate(ctx_parts, axis=0)).astype(BF16).astype(F32)
    dq = (jnp.transpose(jnp.concatenate(dq_parts, axis=0)) * scale).astype(BF16)
    dk = (dk * scale).astype(BF16)
    dv = dv.astype(BF16)
    gated_f = gate * context
    gated = gated_f.astype(BF16)
    att = mm(gated, w_out_ref[...])
    att_ref[...] = att.reshape(n_row, tile_rows, channels).astype(att_ref.dtype)
    d_gate = (d_gated * context * gate * (1.0 - gate)).astype(BF16)
    grads = jnp.concatenate([dq, dk, dv, d_gate], axis=1)
    dn = mm_nt(grads, w_in_ref[...])
    dn_ref[...] = dn.reshape(n_row, tile_rows, channels).astype(dn_ref.dtype)
    gain_s[...] += fold_rows(dn * x_hat)
    x_t = jnp.transpose(x_f).astype(BF16)
    parts_ref[:, : 4 * channels] += mm(x_t, grads)
    gated_t = jnp.transpose(gated_f).astype(BF16)
    parts_ref[:, 4 * channels :] += mm(gated_t, cot)


def layer_kernel(
    heads, valid_ref, pair_ref, cot_ref, gain_ref, bwt_ref, proj_ref,
    atto_ref, pgo_ref, sums_ref, small_ref,
    pair_f, cot_f, x_s, c_s, btile, x_hat_s, normed_s, w_in, xc, cc, ball, bias_s, dbias_s, parts_s, gain_s,
    att_s, dn_s, dno, bterm,
    rbuf, psend, prbuf, zsend, zmate, zopp, zback, parts_c, qr, qs, qp, qmate, qopp, qzs, qhalf, plane_g, outer_g,
    s_fw, r_fw, s_bw, r_bw, s_bo, r_bo, s_bo2, r_bo2, s_bm, r_bm, s_bc, r_bc,
    s_half, r_half, s_opp, r_opp, s_mate, r_mate, s_core, r_core, s_ag, r_ag, s_agc, r_agc,
    s_small, r_small, s_small2, r_small2, s_loc,
):
    row, col, outer, mid, core = place()
    n_row, ncols, tile_rows, channels = x_s.shape
    n_out, n_col = ball.shape[0], ball.shape[3]
    tile_cols = pair_ref.shape[1]
    rows = n_row * tile_rows
    half_out = n_out // 2
    facing = lax.rem(outer + half_out, n_out)
    neighbours = [outer // half_out * half_out + lax.rem(outer + i, half_out) for i in range(1, half_out)]
    other = (outer * 4 + mid * 2 + 1 - core, col)
    w_out_ref = proj_ref.at[4]
    gain = gain_ref[...]

    def along(o):
        return o * 4 + mid * 2 + core, col

    def lanes(h):
        return h // 2, slice(h % 2 * tile_cols, (h % 2 + 1) * tile_cols)

    def turn(c, carry):
        for r in range(n_row):
            at = pl.ds(r * ncols + c, tile_rows, stride=tile_cols)
            x_s[r, c] = pair_f[at, :].astype(BF16)
            c_s[r, c] = cot_f[at, :].astype(BF16)
        return carry

    def send_out(c, carry):
        def peer(i, carry):
            r = lax.rem(row + i, n_row)
            push(x_s.at[r, c], xc.at[c, row], s_fw.at[0], r_fw.at[0, c], (r, col))
            push(c_s.at[r, c], cc.at[c, row], s_fw.at[1], r_fw.at[1, c], (r, col))
            return carry

        return lax.fori_loop(1, n_row, peer, carry)

    def send_back(c, carry):
        def peer(i, carry):
            r = lax.rem(row + i, n_row)
            push(dn_s.at[c, r], dno.at[c, row], s_bw.at[1], r_bw.at[1, c], (r, col))
            push(att_s.at[c, r], atto_ref.at[row, c], s_bw.at[0], r_bw.at[0, c], (r, col))
            return carry

        return lax.fori_loop(1, n_row, peer, carry)

    def turn_and_send(c, carry):
        turn(jnp.minimum(c + 1, ncols - 1), 0)
        return send_out(c, carry)

    barrier, n_others = greet_all()
    for a in range(tile_rows):
        at = slice(a * tile_cols, (a + 1) * tile_cols)
        pair_f[at, :] = pair_ref[a].astype(F32)
        cot_f[at, :] = cot_ref[a].astype(F32)
    lax.fori_loop(0, 2, turn, 0)
    pl.semaphore_wait(barrier, n_others)
    send_out(0, 0)
    for a in range(tile_rows):
        x_hat, _ = norm(pair_f[a * tile_cols : (a + 1) * tile_cols, :])
        normed = (x_hat * gain).astype(BF16)
        x_hat_s[a] = x_hat
        normed_s[a] = normed
        bias_a = mm_nt(bwt_ref[...], normed)
        for h in range(heads):
            p, where = lanes(h)
            btile[p, a : a + 1, where] = bias_a[h : h + 1]
    spot = ball.at[outer, mid, core, col]
    for i, o in enumerate([facing] + neighbours):
        push(btile, spot, s_bo.at[i], r_bo.at[i], along(o))
    own_bias = pltpu.make_async_copy(btile, spot, s_loc.at[0])
    own_bias.start()
    lax.fori_loop(1, 2, turn_and_send, 0)
    dbias_s[...] = jnp.zeros_like(dbias_s)
    for i in range(half_out):
        await_bytes(btile, s_bo.at[i])
        await_bytes(btile, r_bo.at[i])
    spot = ball.at[facing, mid, core, col]
    for i, o in enumerate(neighbours):
        push(spot, spot, s_bo2.at[i], r_bo2.at[i], along(o))
    early = (ncols + 2) // 3
    lax.fori_loop(2, early, turn_and_send, 0)
    own_bias.wait()
    for i in range(half_out - 1):
        await_bytes(spot, s_bo2.at[i])
        await_bytes(spot, r_bo2.at[i])
    mine = ball.at[:, mid, core, col]
    for i, m, k in mates(n_col, mid, col):
        push(mine, mine, s_bm.at[i], r_bm.at[i], (outer * 4 + m * 2 + core, k))
    lax.fori_loop(early, ncols, turn_and_send, 0)
    local = [
        pltpu.make_async_copy(x_s.at[row], xc.at[:, row], s_loc.at[1]),
        pltpu.make_async_copy(c_s.at[row], cc.at[:, row], s_loc.at[2]),
    ]
    for copy in local:
        copy.start()
    parts_s[...] = jnp.zeros_like(parts_s)
    gain_s[...] = jnp.zeros_like(gain_s)
    for m in range(4):
        w_in[:, m * channels : (m + 1) * channels] = proj_ref[m]
    for i in range(2 * n_col - 1):
        await_bytes(mine, s_bm.at[i])
        await_bytes(mine, r_bm.at[i])
    half = ball.at[:, :, core]
    push(half, half, s_bc, r_bc, other)
    await_bytes(half, s_bc)
    await_bytes(half, r_bc)
    for copy in local:
        copy.wait()
    keep_lanes = lax.broadcasted_iota(jnp.int32, (rows, 1), 0) < valid_ref[0]
    for h in range(heads):
        p, where = lanes(h)
        for k in range(n_col):
            block = ball[:, :, :, k, p].reshape(rows, 2 * tile_cols)[:, where]
            bias_s[h, :, k * tile_cols : (k + 1) * tile_cols] = jnp.where(keep_lanes, block, -1000000000.0)

    held = ncols * 1 // 12

    def column(c, carry):
        await_bytes(xc.at[c, pl.ds(0, n_row - 1)], r_fw.at[0, c])
        await_bytes(cc.at[c, pl.ds(0, n_row - 1)], r_fw.at[1, c])

        @pl.when((c > 0) & (c <= ncols - held))
        def _():
            send_back(c - 1, 0)

        attend(
            heads, valid_ref, xc.at[c], cc.at[c], gain, w_in, w_out_ref,
            bias_s, dbias_s, parts_s, gain_s, att_s.at[c], dn_s.at[c],
        )
        return carry

    lax.fori_loop(0, ncols, column, 0)

    n_pairs = heads // 2
    for p in range(n_pairs):
        for h in (2 * p, 2 * p + 1):
            _, where = lanes(h)
            for k in range(n_col):
                block = dbias_s[h, :, k * tile_cols : (k + 1) * tile_cols]
                ball[:, :, :, k, p, :, where] = block.reshape(n_out, 2, 2, tile_rows, tile_cols)
        push(ball.at[:, :, 1 - core, :, p], rbuf.at[p], s_core.at[p], r_core.at[p], other)
    slab = parts_c.shape[3]
    for j in range(5 * channels // slab):
        m, lo = j * slab // channels, j * slab % channels
        first = min(slab, channels - lo)
        piece = parts_s[lo : lo + first, m * channels : (m + 1) * channels]
        if first < slab:
            rest = parts_s[: slab - first, (m + 1) * channels : (m + 2) * channels]
            piece = jnp.concatenate([piece, rest], axis=0)
        parts_c[j // (2 * n_col), j // n_col % 2, j % n_col] = piece
    push(parts_c.at[1 - core], qr, s_core.at[n_pairs], r_core.at[n_pairs], other)
    local = [
        pltpu.make_async_copy(att_s.at[:, row], atto_ref.at[row], s_loc.at[0]),
        pltpu.make_async_copy(dn_s.at[:, row], dno.at[:, row], s_loc.at[1]),
    ]
    for copy in local:
        copy.start()
    for p in range(n_pairs):
        await_bytes(rbuf.at[p], s_core.at[p])
        await_bytes(rbuf.at[p], r_core.at[p])
        for m in range(2):
            for k in range(n_col):
                psend[p, m, k] = (ball[:, m, core, k, p] + rbuf[p, :, m, k]).astype(BF16)
        for i, m, k in mates(n_col, mid, col):
            push(psend.at[p, m, k], prbuf.at[p, i], s_mate.at[p, i], r_mate.at[p, i], (outer * 4 + m * 2 + core, k))
    await_bytes(qr, s_core.at[n_pairs])
    await_bytes(qr, r_core.at[n_pairs])
    qs[...] = parts_c[core] + qr[...]
    for i, m, k in mates(n_col, mid, col):
        push(qs.at[m, k], qp.at[i], s_mate.at[n_pairs, i], r_mate.at[n_pairs, i], (outer * 4 + m * 2 + core, k))
    for p in range(n_pairs):
        own = psend[p, mid, col].astype(F32)
        for i in range(2 * n_col - 1):
            await_bytes(prbuf.at[p, i], s_mate.at[p, i])
            await_bytes(prbuf.at[p, i], r_mate.at[p, i])
            own += prbuf[p, i].astype(F32)
        zsend[:, p] = own
    for i, o in enumerate(neighbours):
        for j, z in enumerate((o, lax.rem(o + half_out, n_out))):
            push(zsend.at[z], zmate.at[i, j], s_half.at[j, i], r_half.at[j, i], along(o))
    mine = qs[mid, col]
    for i in range(2 * n_col - 1):
        await_bytes(qp.at[i], s_mate.at[n_pairs, i])
        await_bytes(qp.at[i], r_mate.at[n_pairs, i])
        mine += qp[i]
    qzs[...] = mine
    for i, o in enumerate(neighbours):
        push(qzs, qmate.at[i], s_half.at[2, i], r_half.at[2, i], along(o))
    first, second = held // 4, (held - held // 4) // 2
    last = held - first - second
    lax.fori_loop(ncols - held, ncols - held + first, send_back, 0)
    total, beyond, sums = zsend[outer], zsend[facing], qzs[...]
    for i in range(half_out - 1):
        for j in range(2):
            await_bytes(zopp, s_half.at[j, i])
            await_bytes(zopp, r_half.at[j, i])
        await_bytes(qzs, s_half.at[2, i])
        await_bytes(qzs, r_half.at[2, i])
        total += zmate[i, 0]
        beyond += zmate[i, 1]
        sums += qmate[i]
    zback[...] = beyond
    qhalf[...] = sums
    push(zback, zopp, s_opp.at[0], r_opp.at[0], along(facing))
    push(qhalf, qopp, s_opp.at[1], r_opp.at[1], along(facing))
    lax.fori_loop(ncols - held + first, ncols - last, send_back, 0)
    for j, ref in ((0, zopp), (1, qopp)):
        await_bytes(ref, s_opp.at[j])
        await_bytes(ref, r_opp.at[j])
    total += zopp[...]
    sums += qopp[...]
    sums_ref[core, mid, col] = sums
    mine = sums_ref.at[core, mid, col]
    for i, m, k in mates(n_col, mid, col):
        push(mine, mine, s_ag.at[i], r_ag.at[i], (outer * 4 + m * 2 + core, k))

    btile[...] = total
    no_heads = jnp.zeros((8 - heads, tile_cols), F32)
    weight_part = jnp.zeros((8, channels), F32)
    gain_part = gain_s[...]
    for a in range(tile_rows):
        d_rows = [btile[p, a : a + 1, where] for p, where in map(lanes, range(heads))]
        d_a = jnp.concatenate(d_rows + [no_heads], axis=0).astype(BF16)
        term = lax.dot_general(d_a, bwt_ref[...], (((0,), (0,)), ((), ())), preferred_element_type=F32)
        bterm[pl.ds(a, tile_cols, stride=tile_rows), :] = term
        weight_part += mm(d_a, normed_s[a])
        gain_part += fold_rows(term * x_hat_s[a])
    at = lax.broadcasted_iota(jnp.int32, (8, channels), 0)
    gain_row = jnp.broadcast_to(jnp.sum(gain_part, axis=0, keepdims=True), (8, channels))
    seat = (mid * n_col + col) * 2 + core
    plane_g[seat] = jnp.where(at < heads, weight_part, jnp.where(at == heads, gain_row, 0.0))
    n_plane = 4 * n_col
    for i in range(1, n_plane):
        there = lax.rem(seat + i, n_plane)
        where = (outer * 4 + there // (2 * n_col) * 2 + lax.rem(there, 2), lax.rem(there // 2, n_col))
        push(plane_g.at[seat], plane_g.at[seat], s_small.at[i - 1], r_small.at[i - 1], where)
    for copy in local:
        copy.wait()

    def finish(c, carry):
        await_bytes(dno.at[c, pl.ds(0, n_row - 1)], r_bw.at[1, c])
        x_hat, inverse = norm(x_s[:, c].astype(F32).reshape(rows, channels))
        block = [bterm[pl.ds(pl.multiple_of((r * ncols + c) * tile_rows, 8), tile_rows), :] for r in range(n_row)]
        g = (dno[c].astype(F32).reshape(rows, channels) + jnp.concatenate(block, axis=0)) * gain
        inner = jnp.mean(g * x_hat, axis=-1, keepdims=True)
        out = inverse * (g - jnp.mean(g, axis=-1, keepdims=True) - x_hat * inner)
        pgo_ref[:, c] = out.reshape(n_row, tile_rows, channels)
        return carry

    lax.fori_loop(0, ncols - held, finish, 0)
    for i in range(n_plane - 1):
        await_bytes(plane_g.at[0], s_small.at[i])
        await_bytes(plane_g.at[0], r_small.at[i])
    outer_g[outer] = jnp.sum(plane_g[...], axis=0)
    for i in range(1, n_out):
        push(outer_g.at[outer], outer_g.at[outer], s_small2.at[i - 1], r_small2.at[i - 1], along(lax.rem(outer + i, n_out)))
    lax.fori_loop(ncols - last, ncols, send_back, 0)
    lax.fori_loop(ncols - held, ncols - last, finish, 0)
    for i in range(2 * n_col - 1):
        await_bytes(mine, s_ag.at[i])
        await_bytes(mine, r_ag.at[i])
    half = sums_ref.at[core]
    push(half, half, s_agc, r_agc, other)
    for i in range(n_out - 1):
        await_bytes(outer_g.at[0], s_small2.at[i])
        await_bytes(outer_g.at[0], r_small2.at[i])
    small_ref[...] = jnp.sum(outer_g[...], axis=0)
    await_bytes(half, s_agc)
    await_bytes(half, r_agc)
    lax.fori_loop(ncols - last, ncols, finish, 0)

    def came_back(c, carry):
        await_bytes(att_s.at[c, pl.ds(0, n_row - 1)], r_bw.at[0, c])
        return carry

    lax.fori_loop(0, ncols, came_back, 0)
    for k in range(2):
        await_bytes(x_s.at[pl.ds(0, n_row - 1)], s_fw.at[k])
        await_bytes(x_s.at[pl.ds(0, n_row - 1)], s_bw.at[k])


def layer(heads, valid_len, pair, cot, gain, bias_rows, projections):
    n_row, n_col = lax.axis_size("row"), lax.axis_size("col")
    tile_rows, tile_cols, channels = pair.shape
    ncols = tile_cols // n_row
    tile = (heads // 2, tile_rows, 2 * tile_cols)
    half_tile = tile[1:]
    n_pairs = heads // 2
    n_out, n_mates, rows = n_row // 4, 2 * n_col - 1, n_row * tile_rows
    half_out = n_out // 2
    slab = (5 * channels // (4 * n_col), channels)
    vmem = pl.BlockSpec(memory_space=VM)
    peers = (n_row, ncols, tile_rows, channels)
    cols = VM((ncols, n_row, tile_rows, channels), BF16)
    flat = VM((tile_rows * tile_cols, channels), F32)
    return pl.pallas_call(
        functools.partial(layer_kernel, heads),
        in_specs=[pl.BlockSpec(memory_space=pltpu.SMEM)] + [vmem] * 5,
        out_specs=[vmem] * 4,
        out_shape=[
            jax.ShapeDtypeStruct(peers, BF16),
            jax.ShapeDtypeStruct(peers, F32),
            jax.ShapeDtypeStruct((2, 2, n_col) + slab, F32),
            jax.ShapeDtypeStruct((8, channels), F32),
        ],
        scratch_shapes=[
            flat, flat, VM(peers, BF16), VM(peers, BF16),
            VM(tile, F32),
            VM(pair.shape, F32),
            VM(pair.shape, BF16),
            VM((channels, 4 * channels), BF16),
            cols, cols,
            VM((n_out, 2, 2, n_col) + tile, F32),
            VM((heads, rows, rows), F32),
            VM((heads, rows, rows), F32),
            VM((channels, 5 * channels), F32),
            VM((8, channels), F32),
            cols, cols, cols,
            flat,
            VM((n_pairs, n_out, 2, n_col) + half_tile, F32),
            VM((n_pairs, 2, n_col, n_out) + half_tile, BF16),
            VM((n_pairs, n_mates, n_out) + half_tile, BF16),
            VM((n_out,) + tile, F32),
            VM((half_out - 1, 2) + tile, F32),
            VM(tile, F32),
            VM(tile, F32),
            VM((2, 2, n_col) + slab, F32),
            VM((2, n_col) + slab, F32),
            VM((2, n_col) + slab, F32),
            VM((n_mates,) + slab, F32),
            VM((half_out - 1,) + slab, F32),
            VM(slab, F32),
            VM(slab, F32),
            VM(slab, F32),
            VM((4 * n_col, 8, channels), F32),
            VM((n_out, 8, channels), F32),
            DMA((2,)), DMA((2, ncols)), DMA((2,)), DMA((2, ncols)),
            DMA((half_out,)), DMA((half_out,)), DMA((half_out - 1,)), DMA((half_out - 1,)),
            DMA((n_mates,)), DMA((n_mates,)), DMA, DMA,
            DMA((3, half_out - 1)), DMA((3, half_out - 1)), DMA((2,)), DMA((2,)),
            DMA((n_pairs + 1, n_mates)), DMA((n_pairs + 1, n_mates)), DMA((n_pairs + 1,)), DMA((n_pairs + 1,)),
            DMA((n_mates,)), DMA((n_mates,)), DMA, DMA,
            DMA((4 * n_col - 1,)), DMA((4 * n_col - 1,)), DMA((n_out - 1,)), DMA((n_out - 1,)), DMA((3,)),
        ],
        compiler_params=pltpu.CompilerParams(
            collective_id=0, has_side_effects=True, vmem_limit_bytes=62 * 1024 * 1024
        ),
    )(valid_len, pair, cot, gain, bias_rows, projections)


def shards(pair, gain, projections, bias_weight, valid_len, out_cotangent):
    tile_rows, tile_cols, channels = pair.shape
    heads = bias_weight.shape[1]

    def to_tile(columns):
        return jnp.swapaxes(columns.reshape(tile_cols, tile_rows, channels), 0, 1)

    bias_rows = jnp.pad(bias_weight.T, ((0, 8 - heads), (0, 0)))
    attended, pair_gradient, sums, small = layer(
        heads, valid_len, pair, out_cotangent, gain[None], bias_rows, projections
    )
    return (
        to_tile(attended),
        to_tile(pair_gradient),
        sums.reshape(5, channels, channels),
        small[:heads].T,
        small[heads],
    )


def solution(mesh):
    placed = (P("row", "col", None), P(), P(), P(), P(), P("row", "col", None))
    return jax.shard_map(
        shards,
        mesh=mesh,
        in_specs=placed,
        out_specs=(P("row", "col", None), P("row", "col", None), P(), P(), P()),
        check_vma=False,
    )
```

```python
import functools

import jax
import jax.numpy as jnp
from jax import lax
from jax.experimental import pallas as pl
from jax.experimental.pallas import tpu as pltpu
from jax.sharding import PartitionSpec as P

EPS = 1e-05
LOG2E = 1.4426950408889634
F32 = jnp.float32
BF16 = jnp.bfloat16


def mm(left, right):
    return lax.dot_general(left, right, (((1,), (0,)), ((), ())), preferred_element_type=F32)


def mm_nt(left, right):
    return lax.dot_general(left, right, (((1,), (1,)), ((), ())), preferred_element_type=F32)


MESH = pl.DeviceIdType.MESH
VM = pltpu.VMEM
DMA = pltpu.SemaphoreType.DMA


def place():
    row, col = lax.axis_index("row"), lax.axis_index("col")
    return row, col, row // 4, lax.rem(row // 2, 2), lax.rem(row, 2)


def greet_all():
    row, col = lax.axis_index("row"), lax.axis_index("col")
    n_row, n_col = lax.axis_size("row"), lax.axis_size("col")
    barrier = pltpu.get_barrier_semaphore()

    def greet(i, carry):
        there = (lax.rem(row + i // n_col, n_row), lax.rem(col + lax.rem(i, n_col), n_col))
        pl.semaphore_signal(barrier, inc=1, device_id=there, device_id_type=MESH)
        return carry

    lax.fori_loop(1, n_row * n_col, greet, 0)
    return barrier, n_row * n_col - 1


def push(src, dst, send, recv, where):
    pltpu.make_async_remote_copy(
        src_ref=src, dst_ref=dst, send_sem=send, recv_sem=recv,
        device_id=where, device_id_type=MESH,
    ).start()


def await_bytes(ref, sem):
    pltpu.make_async_copy(ref, ref, sem).wait()


def mates(n_col, mid, col):
    for i in range(1, 2 * n_col):
        yield i - 1, lax.rem(mid + i // n_col, 2), lax.rem(col + i % n_col, n_col)


def norm(x_f):
    average = jnp.mean(x_f, axis=-1, keepdims=True)
    centered = x_f - average
    inverse = lax.rsqrt(jnp.mean(centered * centered, axis=-1, keepdims=True) + EPS)
    return centered * inverse, inverse


def fold_rows(x_f):
    return jnp.sum(x_f.reshape(-1, 8, x_f.shape[-1]), axis=0)


def prepare(heads, valid_ref, col_ref, gain, w_in_ref, w_out_ref):
    n_row, _, tile_rows, channels = col_ref.shape
    rows = n_row * tile_rows
    keep_lanes = lax.broadcasted_iota(jnp.int32, (rows, 1), 0) < valid_ref[0]
    x_hat, _ = norm(col_ref[:, 0].astype(F32).reshape(rows, channels))
    x_f = x_hat * gain
    cot = col_ref[:, 1].astype(F32).reshape(rows, channels).astype(BF16)
    proj = mm(x_f.astype(BF16), w_in_ref[...])
    query = proj[:, :channels].astype(BF16)
    key_f = jnp.where(keep_lanes, proj[:, channels : 2 * channels], 0.0)
    value_f = proj[:, 2 * channels : 3 * channels]
    gate = jax.nn.sigmoid(proj[:, 3 * channels :])
    d_gated = mm_nt(cot, w_out_ref[...])
    d_context = (d_gated * gate).astype(BF16)
    return x_hat, x_f, cot, query, key_f, value_f, gate, d_gated, d_context


def attend(heads, chosen, query, key_f, value_f, d_context, bias_s, dbias_s):
    rows, channels = query.shape
    width = channels // heads
    scale = width ** (-0.5)
    key, value = key_f.astype(BF16), value_f.astype(BF16)
    key_t = jnp.transpose(key_f).astype(BF16)
    value_t = jnp.transpose(value_f).astype(BF16)
    lane_head = lax.broadcasted_iota(jnp.int32, (rows, channels), 1) // width
    ctx_parts, dq_parts = [], []
    dk = jnp.zeros((rows, channels), F32)
    dv = jnp.zeros((rows, channels), F32)
    for h in chosen:
        mine = lane_head == h
        q_h = jnp.where(mine, query, jnp.zeros_like(query))
        dc_h = jnp.where(mine, d_context, jnp.zeros_like(d_context))
        s = mm_nt(key, q_h) * (scale * LOG2E) + bias_s[h]
        e = jnp.exp2(s - jnp.max(s, axis=0, keepdims=True))
        p = e * (1.0 / jnp.sum(e, axis=0, keepdims=True))
        d_p = mm_nt(value, dc_h)
        delta = jnp.sum(p * d_p, axis=0, keepdims=True)
        ds = p * (d_p - delta)
        dbias_s[h] += ds
        p_b = p.astype(BF16)
        ds_b = ds.astype(BF16)
        ctx_parts.append(mm(value_t[h * width : (h + 1) * width], p_b))
        dq_parts.append(mm(key_t[h * width : (h + 1) * width], ds_b))
        dv += mm(p_b, dc_h)
        dk += mm(ds_b, q_h)
    ctx_t = jnp.concatenate(ctx_parts, axis=0)
    dq_t = jnp.concatenate(dq_parts, axis=0)
    return ctx_t, dq_t, (dk * scale).astype(BF16), dv.astype(BF16)


def conclude(
    heads, x_hat, x_f, cot, gate, d_gated, ctx_t, dq_t, dk, dv,
    w_in_ref, w_out_ref, parts_ref, gain_s, back_ref,
):
    n_row, _, tile_rows, channels = back_ref.shape
    scale = (channels // heads) ** (-0.5)
    context = jnp.transpose(ctx_t).astype(BF16).astype(F32)
    dq = (jnp.transpose(dq_t) * scale).astype(BF16)
    gated_f = gate * context
    gated = gated_f.astype(BF16)
    att = mm(gated, w_out_ref[...])
    back_ref[:, 1] = att.reshape(n_row, tile_rows, channels).astype(BF16)
    d_gate = (d_gated * context * gate * (1.0 - gate)).astype(BF16)
    grads = jnp.concatenate([dq, dk, dv, d_gate], axis=1)
    dn = mm_nt(grads, w_in_ref[...])
    back_ref[:, 0] = dn.reshape(n_row, tile_rows, channels).astype(BF16)
    gain_s[...] += fold_rows(dn * x_hat)
    x_t = jnp.transpose(x_f).astype(BF16)
    parts_ref[:, : 4 * channels] += mm(x_t, grads)
    gated_t = jnp.transpose(gated_f).astype(BF16)
    parts_ref[:, 4 * channels :] += mm(gated_t, cot)


def layer_kernel(
    heads, valid_ref, pair_ref, cot_ref, gain_ref, bwt_ref, proj_ref,
    atto_ref, pgo_ref, sums_ref, small_ref,
    pair_f, cot_f, x_s, btile, x_hat_s, normed_s, w_in, xc, ball, bias_s, dbias_s, parts_s, gain_s,
    back_s, back, bterm,
    rbuf, psend, prbuf, zsend, zmate, zown, zback, zopp, parts_c, qr, qs, qp, qzs, qmate, qhalf, qopp, plane_g, outer_g,
    s_fw, r_fw, s_bw, r_bw, s_ba, r_ba, s_bb, r_bb, s_by, r_by, s_bx, r_bx, s_bc, r_bc, s_loc,
    s_core, r_core, s_mate, r_mate, s_half, r_half, s_opp, r_opp, s_ag, r_ag, s_agc, r_agc,
    s_small, r_small, s_small2, r_small2,
):
    row, col, outer, mid, core = place()
    n_row, ncols, _, tile_rows, channels = x_s.shape
    n_out, n_col = ball.shape[1], ball.shape[4]
    tile_cols = pair_ref.shape[1]
    rows = n_row * tile_rows
    half_out = n_out // 2
    facing = lax.rem(outer + half_out, n_out)
    neighbours = [outer // half_out * half_out + lax.rem(outer + i, half_out) for i in range(1, half_out)]
    n_near, n_mates = half_out - 1, 2 * n_col - 1
    other = (outer * 4 + mid * 2 + 1 - core, col)
    w_out_ref = proj_ref.at[4]
    gain = gain_ref[...]
    group = heads // 2

    def along(o):
        return o * 4 + mid * 2 + core, col

    def mate(m, k):
        return outer * 4 + m * 2 + core, k

    def members(g):
        for n in range(group):
            yield g * group + n, slice(n * tile_cols, (n + 1) * tile_cols)

    def both(ref, send, recv):
        await_bytes(ref, send)
        await_bytes(ref, recv)

    def turn(c, carry):
        for r in range(n_row):
            at = pl.ds(r * ncols + c, tile_rows, stride=tile_cols)
            x_s[r, c, 0] = pair_f[at, :].astype(BF16)
            x_s[r, c, 1] = cot_f[at, :].astype(BF16)
        return carry

    def send_out(c, carry):
        def peer(i, carry):
            r = lax.rem(row + i, n_row)
            push(x_s.at[r, c], xc.at[c, row], s_fw, r_fw.at[0, c], (r, col))
            return carry

        lax.fori_loop(1, n_row, peer, carry)
        pltpu.make_async_copy(x_s.at[row, c], xc.at[c, row], r_fw.at[1, c]).start()
        return carry

    def send_back(c, carry):
        def peer(i, carry):
            r = lax.rem(row + i, n_row)
            push(back_s.at[c, r], back.at[c, row], s_bw, r_bw.at[0, c], (r, col))
            return carry

        lax.fori_loop(1, n_row, peer, carry)
        pltpu.make_async_copy(back_s.at[c, row], back.at[c, row], r_bw.at[1, c]).start()
        return carry

    def send_some_out(lo, hi):
        def one(c, carry):
            turn(jnp.minimum(c + 1, ncols - 1), 0)
            return send_out(c, carry)

        lax.fori_loop(min(lo, ncols), min(hi, ncols), one, 0)

    def bias_facing(g):
        for i, o in enumerate([facing] + neighbours):
            push(btile.at[g], ball.at[g, outer, mid, core, col], s_ba.at[g, i], r_ba.at[g, i], along(o))
        pltpu.make_async_copy(btile.at[g], ball.at[g, outer, mid, core, col], s_loc.at[g]).start()

    def bias_relay(g):
        for i in range(half_out):
            both(btile.at[g], s_ba.at[g, i], r_ba.at[g, i])
        spot = ball.at[g, facing, mid, core, col]
        for i, o in enumerate(neighbours):
            push(spot, spot, s_bb.at[g, i], r_bb.at[g, i], along(o))

    def bias_mid(g):
        await_bytes(btile.at[g], s_loc.at[g])
        for i in range(n_near):
            both(btile.at[g], s_bb.at[g, i], r_bb.at[g, i])
        mine = ball.at[g, :, mid, core, col]
        push(mine, mine, s_by.at[g], r_by.at[g], mate(1 - mid, col))

    def bias_col(g):
        both(ball.at[g, :, mid, core, col], s_by.at[g], r_by.at[g])
        mine = ball.at[g, :, :, core, col]
        for i in range(1, n_col):
            push(mine, mine, s_bx.at[g, i - 1], r_bx.at[g, i - 1], mate(mid, lax.rem(col + i, n_col)))

    def bias_core(g):
        for i in range(n_col - 1):
            both(ball.at[g, :, :, core, col], s_bx.at[g, i], r_bx.at[g, i])
        mine = ball.at[g, :, :, core]
        push(mine, mine, s_bc.at[g], r_bc.at[g], other)

    def bias_done(g):
        both(ball.at[g, :, :, core], s_bc.at[g], r_bc.at[g])
        keep_lanes = lax.broadcasted_iota(jnp.int32, (rows, 1), 0) < valid_ref[0]
        for h, where in members(g):
            for k in range(n_col):
                block = ball[g, :, :, :, k].reshape(rows, group * tile_cols)[:, where]
                bias_s[h, :, k * tile_cols : (k + 1) * tile_cols] = jnp.where(
                    keep_lanes, block * LOG2E, -1000000000.0
                )

    def dbias_core(g):
        for h, where in members(g):
            for k in range(n_col):
                block = dbias_s[h, :, k * tile_cols : (k + 1) * tile_cols]
                ball[g, :, :, :, k, :, where] = block.reshape(n_out, 2, 2, tile_rows, tile_cols)
        push(ball.at[g, :, :, 1 - core], rbuf.at[g], s_core.at[g], r_core.at[g], other)

    def dbias_plane(g):
        both(rbuf.at[g], s_core.at[g], r_core.at[g])
        for m in range(2):
            for k in range(n_col):
                psend[g, m, k] = (ball[g, :, m, core, k] + rbuf[g, :, m, k]).astype(BF16)
        for i, m, k in mates(n_col, mid, col):
            push(psend.at[g, m, k], prbuf.at[g, i], s_mate.at[g, i], r_mate.at[g, i], mate(m, k))

    def dbias_half(g):
        own = psend[g, mid, col].astype(F32)
        for i in range(n_mates):
            both(prbuf.at[g, i], s_mate.at[g, i], r_mate.at[g, i])
            own += prbuf[g, i].astype(F32)
        zsend[g] = own
        for i, o in enumerate(neighbours):
            for j, z in enumerate((o, lax.rem(o + half_out, n_out))):
                push(zsend.at[g, z], zmate.at[g, i, j], s_half.at[g, j, i], r_half.at[g, j, i], along(o))

    def dbias_facing(g):
        total, beyond = zsend[g, outer], zsend[g, facing]
        for i in range(n_near):
            for j in range(2):
                both(zown.at[g], s_half.at[g, j, i], r_half.at[g, j, i])
            total += zmate[g, i, 0]
            beyond += zmate[g, i, 1]
        zown[g] = total
        zback[g] = beyond
        push(zback.at[g], zopp.at[g], s_opp.at[g], r_opp.at[g], along(facing))

    def dbias_done(g):
        both(zopp.at[g], s_opp.at[g], r_opp.at[g])
        btile[g] = zown[g] + zopp[g]

    def parts_core():
        slab = parts_c.shape[3]
        for j in range(5 * channels // slab):
            m, lo = j * slab // channels, j * slab % channels
            first = min(slab, channels - lo)
            piece = parts_s[lo : lo + first, m * channels : (m + 1) * channels]
            if first < slab:
                rest = parts_s[: slab - first, (m + 1) * channels : (m + 2) * channels]
                piece = jnp.concatenate([piece, rest], axis=0)
            parts_c[j // (2 * n_col), j // n_col % 2, j % n_col] = piece
        push(parts_c.at[1 - core], qr, s_core.at[2], r_core.at[2], other)

    def parts_plane():
        both(qr, s_core.at[2], r_core.at[2])
        qs[...] = parts_c[core] + qr[...]
        for i, m, k in mates(n_col, mid, col):
            push(qs.at[m, k], qp.at[i], s_mate.at[2, i], r_mate.at[2, i], mate(m, k))

    def parts_half():
        mine = qs[mid, col]
        for i in range(n_mates):
            both(qp.at[i], s_mate.at[2, i], r_mate.at[2, i])
            mine += qp[i]
        qzs[...] = mine
        for i, o in enumerate(neighbours):
            push(qzs, qmate.at[i], s_half.at[2, 0, i], r_half.at[2, 0, i], along(o))

    def parts_facing():
        mine = qzs[...]
        for i in range(n_near):
            both(qzs, s_half.at[2, 0, i], r_half.at[2, 0, i])
            mine += qmate[i]
        qhalf[...] = mine
        push(qhalf, qopp, s_opp.at[2], r_opp.at[2], along(facing))

    def parts_back():
        both(qopp, s_opp.at[2], r_opp.at[2])
        sums_ref[core, mid, col] = qhalf[...] + qopp[...]
        mine = sums_ref.at[core, mid, col]
        for i, m, k in mates(n_col, mid, col):
            push(mine, mine, s_ag.at[i], r_ag.at[i], mate(m, k))

    def parts_back_core():
        for i in range(n_mates):
            both(sums_ref.at[core, mid, col], s_ag.at[i], r_ag.at[i])
        push(sums_ref.at[core], sums_ref.at[core], s_agc, r_agc, other)

    barrier, n_others = greet_all()
    for a in range(tile_rows):
        at = slice(a * tile_cols, (a + 1) * tile_cols)
        pair_f[at, :] = pair_ref[a].astype(F32)
        cot_f[at, :] = cot_ref[a].astype(F32)
    for a in range(tile_rows):
        x_hat, _ = norm(pair_f[a * tile_cols : (a + 1) * tile_cols, :])
        normed = (x_hat * gain).astype(BF16)
        x_hat_s[a] = x_hat
        normed_s[a] = normed
        bias_a = mm_nt(bwt_ref[...], normed)
        for g in range(2):
            for h, where in members(g):
                btile[g, a : a + 1, where] = bias_a[h : h + 1]
    pl.semaphore_wait(barrier, n_others)
    bias_facing(0)
    bias_facing(1)
    turn(0, 0)
    bias_relay(0)
    send_some_out(0, 1)
    bias_relay(1)
    send_some_out(1, 2)
    dbias_s[...] = jnp.zeros_like(dbias_s)
    parts_s[...] = jnp.zeros_like(parts_s)
    gain_s[...] = jnp.zeros_like(gain_s)
    for m in range(4):
        w_in[:, m * channels : (m + 1) * channels] = proj_ref[m]
    bias_mid(0)
    send_some_out(2, 3)
    bias_col(0)
    bias_mid(1)
    send_some_out(3, 5)
    bias_col(1)
    send_some_out(5, ncols)
    bias_core(0)
    bias_core(1)
    bias_done(0)
    bias_done(1)

    def step_of(t, carry):
        await_bytes(xc.at[t, pl.ds(0, n_row - 1)], r_fw.at[0, t])
        await_bytes(xc.at[t, 0], r_fw.at[1, t])

        @pl.when((t > 0) & (t < ncols - 1))
        def _():
            send_back(t - 1, 0)

        x_hat, x_f, cot, query, key_f, value_f, gate, d_gated, d_context = prepare(
            heads, valid_ref, xc.at[t], gain, w_in, w_out_ref
        )
        ctx_t, dq_t, dk, dv = attend(heads, range(heads), query, key_f, value_f, d_context, bias_s, dbias_s)
        conclude(
            heads, x_hat, x_f, cot, gate, d_gated, ctx_t, dq_t, dk, dv,
            w_in, w_out_ref, parts_s, gain_s, back_s.at[t],
        )
        return carry

    lax.fori_loop(0, ncols, step_of, 0)

    def arrive(c, carry):
        await_bytes(back.at[c, pl.ds(0, n_row - 1)], r_bw.at[0, c])
        await_bytes(back.at[c, 0], r_bw.at[1, c])
        return carry

    dbias_core(0)
    dbias_core(1)
    parts_core()
    dbias_plane(0)
    dbias_plane(1)
    parts_plane()
    dbias_half(0)
    dbias_half(1)
    parts_half()
    send_back(ncols - 2, 0)
    dbias_facing(0)
    dbias_facing(1)
    parts_facing()
    send_back(ncols - 1, 0)
    dbias_done(0)
    dbias_done(1)
    parts_back()

    no_heads = jnp.zeros((8 - heads, tile_cols), F32)
    weight_part = jnp.zeros((8, channels), F32)
    gain_part = gain_s[...]
    for a in range(tile_rows):
        d_rows = [btile[g, a : a + 1, where] for g in range(2) for _, where in members(g)]
        d_a = jnp.concatenate(d_rows + [no_heads], axis=0).astype(BF16)
        term = lax.dot_general(d_a, bwt_ref[...], (((0,), (0,)), ((), ())), preferred_element_type=F32)
        bterm[pl.ds(a, tile_cols, stride=tile_rows), :] = term
        weight_part += mm(d_a, normed_s[a])
        gain_part += fold_rows(term * x_hat_s[a])
    at = lax.broadcasted_iota(jnp.int32, (8, channels), 0)
    gain_row = jnp.broadcast_to(jnp.sum(gain_part, axis=0, keepdims=True), (8, channels))
    seat = (mid * n_col + col) * 2 + core
    plane_g[seat] = jnp.where(at < heads, weight_part, jnp.where(at == heads, gain_row, 0.0))
    n_plane = 4 * n_col
    for i in range(1, n_plane):
        there = lax.rem(seat + i, n_plane)
        where = (outer * 4 + there // (2 * n_col) * 2 + lax.rem(there, 2), lax.rem(there // 2, n_col))
        push(plane_g.at[seat], plane_g.at[seat], s_small.at[i - 1], r_small.at[i - 1], where)

    def finish(c, carry):
        x_hat, inverse = norm(x_s[:, c, 0].astype(F32).reshape(rows, channels))
        block = [bterm[pl.ds(pl.multiple_of((r * ncols + c) * tile_rows, 8), tile_rows), :] for r in range(n_row)]
        g = (back[c, :, 0].astype(F32).reshape(rows, channels) + jnp.concatenate(block, axis=0)) * gain
        inner = jnp.mean(g * x_hat, axis=-1, keepdims=True)
        out = inverse * (g - jnp.mean(g, axis=-1, keepdims=True) - x_hat * inner)
        pgo_ref[:, c] = out.reshape(n_row, tile_rows, channels)
        atto_ref[:, c] = back[c, :, 1]
        return carry

    def arrive_and_finish(c, carry):
        return finish(c, arrive(c, carry))

    lax.fori_loop(0, ncols // 3, arrive_and_finish, 0)
    for i in range(n_plane - 1):
        both(plane_g.at[0], s_small.at[i], r_small.at[i])
    outer_g[outer] = jnp.sum(plane_g[...], axis=0)
    for i in range(1, n_out):
        push(outer_g.at[outer], outer_g.at[outer], s_small2.at[i - 1], r_small2.at[i - 1], along(lax.rem(outer + i, n_out)))
    parts_back_core()
    lax.fori_loop(ncols // 3, ncols, arrive_and_finish, 0)
    for i in range(n_out - 1):
        both(outer_g.at[0], s_small2.at[i], r_small2.at[i])
    small_ref[...] = jnp.sum(outer_g[...], axis=0)
    both(sums_ref.at[core], s_agc, r_agc)
    await_bytes(x_s.at[pl.ds(0, n_row - 1)], s_fw)
    await_bytes(x_s.at[pl.ds(0, n_row - 1)], s_bw)


def layer(heads, valid_len, pair, cot, gain, bias_rows, projections):
    n_row, n_col = lax.axis_size("row"), lax.axis_size("col")
    tile_rows, tile_cols, channels = pair.shape
    ncols = tile_cols // n_row
    tile = (tile_rows, heads // 2 * tile_cols)
    n_out, n_mates, rows = n_row // 4, 2 * n_col - 1, n_row * tile_rows
    half_out = n_out // 2
    slab = (5 * channels // (4 * n_col), channels)
    vmem = pl.BlockSpec(memory_space=VM)
    peers = (n_row, ncols, tile_rows, channels)
    cols = VM((ncols, n_row, 2, tile_rows, channels), BF16)
    flat = VM((tile_rows * tile_cols, channels), F32)

    def pairs(*shape):
        return [DMA(shape), DMA(shape)]

    return pl.pallas_call(
        functools.partial(layer_kernel, heads),
        in_specs=[pl.BlockSpec(memory_space=pltpu.SMEM)] + [vmem] * 5,
        out_specs=[vmem] * 4,
        out_shape=[
            jax.ShapeDtypeStruct(peers, BF16),
            jax.ShapeDtypeStruct(peers, F32),
            jax.ShapeDtypeStruct((2, 2, n_col) + slab, F32),
            jax.ShapeDtypeStruct((8, channels), F32),
        ],
        scratch_shapes=[
            flat, flat, VM((n_row, ncols, 2, tile_rows, channels), BF16),
            VM((2,) + tile, F32),
            VM(pair.shape, F32),
            VM(pair.shape, BF16),
            VM((channels, 4 * channels), BF16),
            cols,
            VM((2, n_out, 2, 2, n_col) + tile, F32),
            VM((heads, rows, rows), F32),
            VM((heads, rows, rows), F32),
            VM((channels, 5 * channels), F32),
            VM((8, channels), F32),
            cols, cols,
            flat,
            VM((2, n_out, 2, n_col) + tile, F32),
            VM((2, 2, n_col, n_out) + tile, BF16),
            VM((2, n_mates, n_out) + tile, BF16),
            VM((2, n_out) + tile, F32),
            VM((2, half_out - 1, 2) + tile, F32),
            VM((2,) + tile, F32),
            VM((2,) + tile, F32),
            VM((2,) + tile, F32),
            VM((2, 2, n_col) + slab, F32),
            VM((2, n_col) + slab, F32),
            VM((2, n_col) + slab, F32),
            VM((n_mates,) + slab, F32),
            VM(slab, F32),
            VM((half_out - 1,) + slab, F32),
            VM(slab, F32),
            VM(slab, F32),
            VM((4 * n_col, 8, channels), F32),
            VM((n_out, 8, channels), F32),
            DMA, DMA((2, ncols)), DMA, DMA((2, ncols)),
            *pairs(2, half_out), *pairs(2, half_out - 1), *pairs(2), *pairs(2, n_col - 1), *pairs(2), DMA((2,)),
            *pairs(3), *pairs(3, n_mates), *pairs(3, 2, half_out - 1), *pairs(3),
            *pairs(n_mates), DMA, DMA, *pairs(4 * n_col - 1), *pairs(n_out - 1),
        ],
        compiler_params=pltpu.CompilerParams(
            collective_id=0, has_side_effects=True, vmem_limit_bytes=63 * 1024 * 1024
        ),
    )(valid_len, pair, cot, gain, bias_rows, projections)


def shards(pair, gain, projections, bias_weight, valid_len, out_cotangent):
    tile_rows, tile_cols, channels = pair.shape
    heads = bias_weight.shape[1]

    def to_tile(columns):
        return jnp.swapaxes(columns.reshape(tile_cols, tile_rows, channels), 0, 1)

    bias_rows = jnp.pad(bias_weight.T, ((0, 8 - heads), (0, 0)))
    attended, pair_gradient, sums, small = layer(
        heads, valid_len, pair, out_cotangent, gain[None], bias_rows, projections
    )
    return (
        to_tile(attended),
        to_tile(pair_gradient),
        sums.reshape(5, channels, channels),
        small[:heads].T,
        small[heads],
    )


def solution(mesh):
    placed = (P("row", "col", None), P(), P(), P(), P(), P("row", "col", None))
    return jax.shard_map(
        shards,
        mesh=mesh,
        in_specs=placed,
        out_specs=(P("row", "col", None), P("row", "col", None), P(), P(), P()),
        check_vma=False,
    )
```

```python
import functools

import jax
import jax.numpy as jnp
from jax import lax
from jax.experimental import pallas as pl
from jax.experimental.pallas import tpu as pltpu
from jax.sharding import PartitionSpec as P

EPS = 1e-05
LOG2E = 1.4426950408889634
F32 = jnp.float32
BF16 = jnp.bfloat16


def mm(left, right):
    return lax.dot_general(left, right, (((1,), (0,)), ((), ())), preferred_element_type=F32)


def mm_nt(left, right):
    return lax.dot_general(left, right, (((1,), (1,)), ((), ())), preferred_element_type=F32)


MESH = pl.DeviceIdType.MESH
VM = pltpu.VMEM
DMA = pltpu.SemaphoreType.DMA


def place():
    row, col = lax.axis_index("row"), lax.axis_index("col")
    return row, col, row // 4, lax.rem(row // 2, 2), lax.rem(row, 2)


def greet_all():
    row, col = lax.axis_index("row"), lax.axis_index("col")
    n_row, n_col = lax.axis_size("row"), lax.axis_size("col")
    barrier = pltpu.get_barrier_semaphore()

    def greet(i, carry):
        there = (lax.rem(row + i // n_col, n_row), lax.rem(col + lax.rem(i, n_col), n_col))
        pl.semaphore_signal(barrier, inc=1, device_id=there, device_id_type=MESH)
        return carry

    lax.fori_loop(1, n_row * n_col, greet, 0)
    return barrier, n_row * n_col - 1


def push(src, dst, send, recv, where):
    pltpu.make_async_remote_copy(
        src_ref=src, dst_ref=dst, send_sem=send, recv_sem=recv,
        device_id=where, device_id_type=MESH,
    ).start()


def await_bytes(ref, sem):
    pltpu.make_async_copy(ref, ref, sem).wait()


def mates(n_col, mid, col):
    for i in range(1, 2 * n_col):
        yield i - 1, lax.rem(mid + i // n_col, 2), lax.rem(col + i % n_col, n_col)


def norm(x_f):
    average = jnp.mean(x_f, axis=-1, keepdims=True)
    centered = x_f - average
    inverse = lax.rsqrt(jnp.mean(centered * centered, axis=-1, keepdims=True) + EPS)
    return centered * inverse, inverse


def fold_rows(x_f):
    return jnp.sum(x_f.reshape(-1, 8, x_f.shape[-1]), axis=0)


def prepare(heads, valid_ref, col_ref, gain, w_in_ref, w_out_ref):
    n_row, _, tile_rows, channels = col_ref.shape
    rows = n_row * tile_rows
    keep_lanes = lax.broadcasted_iota(jnp.int32, (rows, 1), 0) < valid_ref[0]
    x_hat, _ = norm(col_ref[:, 0].astype(F32).reshape(rows, channels))
    x_f = x_hat * gain
    cot = col_ref[:, 1].astype(F32).reshape(rows, channels).astype(BF16)
    proj = mm(x_f.astype(BF16), w_in_ref[...])
    query = proj[:, :channels].astype(BF16)
    key_f = jnp.where(keep_lanes, proj[:, channels : 2 * channels], 0.0)
    value_f = proj[:, 2 * channels : 3 * channels]
    gate = jax.nn.sigmoid(proj[:, 3 * channels :])
    d_gated = mm_nt(cot, w_out_ref[...])
    d_context = (d_gated * gate).astype(BF16)
    return x_hat, x_f, cot, query, key_f, value_f, gate, d_gated, d_context


def attend(heads, chosen, query, key_f, value_f, d_context, bias_s, dbias_s):
    rows, channels = query.shape
    width = channels // heads
    scale = width ** (-0.5)
    key, value = key_f.astype(BF16), value_f.astype(BF16)
    key_t = jnp.transpose(key_f).astype(BF16)
    value_t = jnp.transpose(value_f).astype(BF16)
    lane_head = lax.broadcasted_iota(jnp.int32, (rows, channels), 1) // width
    ctx_parts, dq_parts = [], []
    dk = jnp.zeros((rows, channels), F32)
    dv = jnp.zeros((rows, channels), F32)
    for h in chosen:
        mine = lane_head == h
        q_h = jnp.where(mine, query, jnp.zeros_like(query))
        dc_h = jnp.where(mine, d_context, jnp.zeros_like(d_context))
        s = mm_nt(key, q_h) * (scale * LOG2E) + bias_s[h]
        e = jnp.exp2(s - jnp.max(s, axis=0, keepdims=True))
        p = e * (1.0 / jnp.sum(e, axis=0, keepdims=True))
        d_p = mm_nt(value, dc_h)
        delta = jnp.sum(p * d_p, axis=0, keepdims=True)
        ds = p * (d_p - delta)
        dbias_s[h] += ds
        p_b = p.astype(BF16)
        ds_b = ds.astype(BF16)
        ctx_parts.append(mm(value_t[h * width : (h + 1) * width], p_b))
        dq_parts.append(mm(key_t[h * width : (h + 1) * width], ds_b))
        dv += mm(p_b, dc_h)
        dk += mm(ds_b, q_h)
    ctx_t = jnp.concatenate(ctx_parts, axis=0)
    dq_t = jnp.concatenate(dq_parts, axis=0)
    return ctx_t, dq_t, (dk * scale).astype(BF16), dv.astype(BF16)


def conclude(
    heads, x_hat, x_f, cot, gate, d_gated, ctx_t, dq_t, dk, dv,
    w_in_ref, w_out_ref, parts_ref, gain_s, back_ref,
):
    n_row, _, tile_rows, channels = back_ref.shape
    scale = (channels // heads) ** (-0.5)
    context = jnp.transpose(ctx_t).astype(BF16).astype(F32)
    dq = (jnp.transpose(dq_t) * scale).astype(BF16)
    gated_f = gate * context
    gated = gated_f.astype(BF16)
    att = mm(gated, w_out_ref[...])
    back_ref[:, 1] = att.reshape(n_row, tile_rows, channels).astype(BF16)
    d_gate = (d_gated * context * gate * (1.0 - gate)).astype(BF16)
    grads = jnp.concatenate([dq, dk, dv, d_gate], axis=1)
    dn = mm_nt(grads, w_in_ref[...])
    back_ref[:, 0] = dn.reshape(n_row, tile_rows, channels).astype(BF16)
    gain_s[...] += fold_rows(dn * x_hat)
    x_t = jnp.transpose(x_f).astype(BF16)
    parts_ref[:, : 4 * channels] += mm(x_t, grads)
    gated_t = jnp.transpose(gated_f).astype(BF16)
    parts_ref[:, 4 * channels :] += mm(gated_t, cot)


def layer_kernel(
    heads, valid_ref, pair_ref, cot_ref, gain_ref, bwt_ref, proj_ref,
    atto_ref, pgo_ref, sums_ref, small_ref, gain_out_ref,
    pair_f, cot_f, x_s, btile, x_hat_s, normed_s, w_in, xc, ball, bias_s, dbias_s, parts_s, gain_s,
    back_s, back, bterm,
    rbuf, psend, prbuf, zsend, zmate, zown, zback, zopp, parts_c, qr, qs, qp, qzs, qmate, qhalf, qopp, plane_g, outer_g,
    s_fw, r_fw, s_bw, r_bw, s_ba, r_ba, s_bb, r_bb, s_by, r_by, s_bx, r_bx, s_bc, r_bc, s_loc,
    s_core, r_core, s_mate, r_mate, s_half, r_half, s_opp, r_opp, s_ag, r_ag, s_agc, r_agc,
    s_small, r_small, s_small2, r_small2,
):
    row, col, outer, mid, core = place()
    n_row, ncols, _, tile_rows, channels = x_s.shape
    n_out, n_col = ball.shape[1], ball.shape[4]
    tile_cols = pair_ref.shape[1]
    rows = n_row * tile_rows
    half_out = n_out // 2
    facing = lax.rem(outer + half_out, n_out)
    neighbours = [outer // half_out * half_out + lax.rem(outer + i, half_out) for i in range(1, half_out)]
    n_near, n_mates = half_out - 1, 2 * n_col - 1
    other = (outer * 4 + mid * 2 + 1 - core, col)
    w_out_ref = proj_ref.at[4]
    gain = gain_ref[...]
    group = heads // 2

    def along(o):
        return o * 4 + mid * 2 + core, col

    def mate(m, k):
        return outer * 4 + m * 2 + core, k

    def members(g):
        for n in range(group):
            yield g * group + n, slice(n * tile_cols, (n + 1) * tile_cols)

    def both(ref, send, recv):
        await_bytes(ref, send)
        await_bytes(ref, recv)

    def turn(c, carry):
        for r in range(n_row):
            at = pl.ds(r * ncols + c, tile_rows, stride=tile_cols)
            x_s[r, c, 0] = pair_f[at, :].astype(BF16)
            x_s[r, c, 1] = cot_f[at, :].astype(BF16)
        return carry

    def send_out(c, carry):
        def peer(i, carry):
            r = lax.rem(row + i, n_row)
            push(x_s.at[r, c], xc.at[c, row], s_fw, r_fw.at[0, c], (r, col))
            return carry

        lax.fori_loop(1, n_row, peer, carry)
        pltpu.make_async_copy(x_s.at[row, c], xc.at[c, row], r_fw.at[1, c]).start()
        return carry

    def send_back(c, carry):
        def peer(i, carry):
            r = lax.rem(row + i, n_row)
            push(back_s.at[c, r], back.at[c, row], s_bw, r_bw.at[0, c], (r, col))
            return carry

        lax.fori_loop(1, n_row, peer, carry)
        pltpu.make_async_copy(back_s.at[c, row], back.at[c, row], r_bw.at[1, c]).start()
        return carry

    def send_some_out(lo, hi):
        def one(c, carry):
            turn(jnp.minimum(c + 1, ncols - 1), 0)
            return send_out(c, carry)

        lax.fori_loop(min(lo, ncols), min(hi, ncols), one, 0)

    def bias_facing(g):
        for i, o in enumerate([facing] + neighbours):
            push(btile.at[g], ball.at[g, outer, mid, core, col], s_ba.at[g, i], r_ba.at[g, i], along(o))
        pltpu.make_async_copy(btile.at[g], ball.at[g, outer, mid, core, col], s_loc.at[g]).start()

    def bias_relay(g):
        for i in range(half_out):
            both(btile.at[g], s_ba.at[g, i], r_ba.at[g, i])
        spot = ball.at[g, facing, mid, core, col]
        for i, o in enumerate(neighbours):
            push(spot, spot, s_bb.at[g, i], r_bb.at[g, i], along(o))

    def bias_mid(g):
        await_bytes(btile.at[g], s_loc.at[g])
        for i in range(n_near):
            both(btile.at[g], s_bb.at[g, i], r_bb.at[g, i])
        mine = ball.at[g, :, mid, core, col]
        push(mine, mine, s_by.at[g], r_by.at[g], mate(1 - mid, col))

    def bias_col(g):
        both(ball.at[g, :, mid, core, col], s_by.at[g], r_by.at[g])
        mine = ball.at[g, :, :, core, col]
        for i in range(1, n_col):
            push(mine, mine, s_bx.at[g, i - 1], r_bx.at[g, i - 1], mate(mid, lax.rem(col + i, n_col)))

    def bias_core(g):
        for i in range(n_col - 1):
            both(ball.at[g, :, :, core, col], s_bx.at[g, i], r_bx.at[g, i])
        mine = ball.at[g, :, :, core]
        push(mine, mine, s_bc.at[g], r_bc.at[g], other)

    def bias_done(g):
        both(ball.at[g, :, :, core], s_bc.at[g], r_bc.at[g])
        keep_lanes = lax.broadcasted_iota(jnp.int32, (rows, 1), 0) < valid_ref[0]
        for h, where in members(g):
            for k in range(n_col):
                block = ball[g, :, :, :, k].reshape(rows, group * tile_cols)[:, where]
                bias_s[h, :, k * tile_cols : (k + 1) * tile_cols] = jnp.where(
                    keep_lanes, block * LOG2E, -1000000000.0
                )

    def dbias_core(g):
        for h, where in members(g):
            for k in range(n_col):
                block = dbias_s[h, :, k * tile_cols : (k + 1) * tile_cols]
                ball[g, :, :, :, k, :, where] = block.reshape(n_out, 2, 2, tile_rows, tile_cols)
        push(ball.at[g, :, :, 1 - core], rbuf.at[g], s_core.at[g], r_core.at[g], other)

    def dbias_plane(g):
        both(rbuf.at[g], s_core.at[g], r_core.at[g])
        for m in range(2):
            for k in range(n_col):
                psend[g, m, k] = (ball[g, :, m, core, k] + rbuf[g, :, m, k]).astype(BF16)
        for i, m, k in mates(n_col, mid, col):
            push(psend.at[g, m, k], prbuf.at[g, i], s_mate.at[g, i], r_mate.at[g, i], mate(m, k))

    def dbias_half(g):
        own = psend[g, mid, col].astype(F32)
        for i in range(n_mates):
            both(prbuf.at[g, i], s_mate.at[g, i], r_mate.at[g, i])
            own += prbuf[g, i].astype(F32)
        zsend[g] = own
        for i, o in enumerate(neighbours):
            for j, z in enumerate((o, lax.rem(o + half_out, n_out))):
                push(zsend.at[g, z], zmate.at[g, i, j], s_half.at[g, j, i], r_half.at[g, j, i], along(o))

    def dbias_facing(g):
        total, beyond = zsend[g, outer], zsend[g, facing]
        for i in range(n_near):
            for j in range(2):
                both(zown.at[g], s_half.at[g, j, i], r_half.at[g, j, i])
            total += zmate[g, i, 0]
            beyond += zmate[g, i, 1]
        zown[g] = total
        zback[g] = beyond
        push(zback.at[g], zopp.at[g], s_opp.at[g], r_opp.at[g], along(facing))

    def dbias_done(g):
        both(zopp.at[g], s_opp.at[g], r_opp.at[g])
        btile[g] = zown[g] + zopp[g]

    def parts_core():
        slab = parts_c.shape[3]
        for j in range(5 * channels // slab):
            m, lo = j * slab // channels, j * slab % channels
            first = min(slab, channels - lo)
            piece = parts_s[lo : lo + first, m * channels : (m + 1) * channels]
            if first < slab:
                rest = parts_s[: slab - first, (m + 1) * channels : (m + 2) * channels]
                piece = jnp.concatenate([piece, rest], axis=0)
            parts_c[j // (2 * n_col), j // n_col % 2, j % n_col] = piece
        push(parts_c.at[1 - core], qr, s_core.at[2], r_core.at[2], other)

    def parts_plane():
        both(qr, s_core.at[2], r_core.at[2])
        qs[...] = parts_c[core] + qr[...]
        for i, m, k in mates(n_col, mid, col):
            push(qs.at[m, k], qp.at[i], s_mate.at[2, i], r_mate.at[2, i], mate(m, k))

    def parts_half():
        mine = qs[mid, col]
        for i in range(n_mates):
            both(qp.at[i], s_mate.at[2, i], r_mate.at[2, i])
            mine += qp[i]
        qzs[...] = mine
        for i, o in enumerate(neighbours):
            push(qzs, qmate.at[i], s_half.at[2, 0, i], r_half.at[2, 0, i], along(o))

    def parts_facing():
        mine = qzs[...]
        for i in range(n_near):
            both(qzs, s_half.at[2, 0, i], r_half.at[2, 0, i])
            mine += qmate[i]
        qhalf[...] = mine
        push(qhalf, qopp, s_opp.at[2], r_opp.at[2], along(facing))

    def parts_back():
        both(qopp, s_opp.at[2], r_opp.at[2])
        sums_ref[core, mid, col] = qhalf[...] + qopp[...]
        mine = sums_ref.at[core, mid, col]
        for i, m, k in mates(n_col, mid, col):
            push(mine, mine, s_ag.at[i], r_ag.at[i], mate(m, k))

    def parts_back_core():
        for i in range(n_mates):
            both(sums_ref.at[core, mid, col], s_ag.at[i], r_ag.at[i])
        push(sums_ref.at[core], sums_ref.at[core], s_agc, r_agc, other)

    barrier, n_others = greet_all()
    for a in range(tile_rows):
        at = slice(a * tile_cols, (a + 1) * tile_cols)
        pair_f[at, :] = pair_ref[a].astype(F32)
        cot_f[at, :] = cot_ref[a].astype(F32)
    for a in range(tile_rows):
        x_hat, _ = norm(pair_f[a * tile_cols : (a + 1) * tile_cols, :])
        normed = (x_hat * gain).astype(BF16)
        x_hat_s[a] = x_hat
        normed_s[a] = normed
        bias_a = mm_nt(bwt_ref[...], normed)
        for g in range(2):
            for h, where in members(g):
                btile[g, a : a + 1, where] = bias_a[h : h + 1]
    pl.semaphore_wait(barrier, n_others)
    bias_facing(0)
    bias_facing(1)
    turn(0, 0)
    bias_relay(0)
    send_some_out(0, 1)
    bias_relay(1)
    send_some_out(1, 2)
    dbias_s[...] = jnp.zeros_like(dbias_s)
    parts_s[...] = jnp.zeros_like(parts_s)
    gain_s[...] = jnp.zeros_like(gain_s)
    for m in range(4):
        w_in[:, m * channels : (m + 1) * channels] = proj_ref[m]
    bias_mid(0)
    send_some_out(2, 3)
    bias_col(0)
    bias_mid(1)
    send_some_out(3, 5)
    bias_col(1)
    send_some_out(5, ncols)
    bias_core(0)
    bias_core(1)
    bias_done(0)
    bias_done(1)

    def step_of(t, carry):
        await_bytes(xc.at[t, pl.ds(0, n_row - 1)], r_fw.at[0, t])
        await_bytes(xc.at[t, 0], r_fw.at[1, t])

        @pl.when((t > 0) & (t < ncols - 1))
        def _():
            send_back(t - 1, 0)

        x_hat, x_f, cot, query, key_f, value_f, gate, d_gated, d_context = prepare(
            heads, valid_ref, xc.at[t], gain, w_in, w_out_ref
        )
        ctx_t, dq_t, dk, dv = attend(heads, range(heads), query, key_f, value_f, d_context, bias_s, dbias_s)
        conclude(
            heads, x_hat, x_f, cot, gate, d_gated, ctx_t, dq_t, dk, dv,
            w_in, w_out_ref, parts_s, gain_s, back_s.at[t],
        )
        return carry

    lax.fori_loop(0, ncols, step_of, 0)

    def arrive(c, carry):
        await_bytes(back.at[c, pl.ds(0, n_row - 1)], r_bw.at[0, c])
        await_bytes(back.at[c, 0], r_bw.at[1, c])
        return carry

    dbias_core(0)
    dbias_core(1)
    parts_core()
    dbias_plane(0)
    dbias_plane(1)
    parts_plane()
    dbias_half(0)
    dbias_half(1)
    parts_half()
    send_back(ncols - 2, 0)
    dbias_facing(0)
    dbias_facing(1)
    parts_facing()
    send_back(ncols - 1, 0)
    dbias_done(0)
    dbias_done(1)
    parts_back()

    no_heads = jnp.zeros((8 - heads, tile_cols), F32)
    weight_part = jnp.zeros((8, channels), F32)
    gain_part = gain_s[...]
    for a in range(tile_rows):
        d_rows = [btile[g, a : a + 1, where] for g in range(2) for _, where in members(g)]
        d_a = jnp.concatenate(d_rows + [no_heads], axis=0).astype(BF16)
        term = lax.dot_general(d_a, bwt_ref[...], (((0,), (0,)), ((), ())), preferred_element_type=F32)
        bterm[pl.ds(a, tile_cols, stride=tile_rows), :] = term
        weight_part += mm(d_a, normed_s[a])
        gain_part += fold_rows(term * x_hat_s[a])
    at = lax.broadcasted_iota(jnp.int32, (8, channels), 0)
    gain_row = jnp.broadcast_to(jnp.sum(gain_part, axis=0, keepdims=True), (8, channels))
    seat = (mid * n_col + col) * 2 + core
    plane_g[seat] = jnp.where(at < heads, weight_part, jnp.where(at == heads, gain_row, 0.0))
    n_plane = 4 * n_col
    for i in range(1, n_plane):
        there = lax.rem(seat + i, n_plane)
        where = (outer * 4 + there // (2 * n_col) * 2 + lax.rem(there, 2), lax.rem(there // 2, n_col))
        push(plane_g.at[seat], plane_g.at[seat], s_small.at[i - 1], r_small.at[i - 1], where)

    def finish(c, carry):
        x_hat, inverse = norm(x_s[:, c, 0].astype(F32).reshape(rows, channels))
        block = [bterm[pl.ds(pl.multiple_of((r * ncols + c) * tile_rows, 8), tile_rows), :] for r in range(n_row)]
        g = (back[c, :, 0].astype(F32).reshape(rows, channels) + jnp.concatenate(block, axis=0)) * gain
        inner = jnp.mean(g * x_hat, axis=-1, keepdims=True)
        out = inverse * (g - jnp.mean(g, axis=-1, keepdims=True) - x_hat * inner)
        pgo_ref[:, c] = out.reshape(n_row, tile_rows, channels)
        atto_ref[:, c] = back[c, :, 1]
        return carry

    def arrive_and_finish(c, carry):
        return finish(c, arrive(c, carry))

    lax.fori_loop(0, ncols // 3, arrive_and_finish, 0)
    for i in range(n_plane - 1):
        both(plane_g.at[0], s_small.at[i], r_small.at[i])
    outer_g[outer] = jnp.sum(plane_g[...], axis=0)
    for i in range(1, n_out):
        push(outer_g.at[outer], outer_g.at[outer], s_small2.at[i - 1], r_small2.at[i - 1], along(lax.rem(outer + i, n_out)))
    parts_back_core()
    lax.fori_loop(ncols // 3, ncols, arrive_and_finish, 0)
    for i in range(n_out - 1):
        both(outer_g.at[0], s_small2.at[i], r_small2.at[i])
    small = jnp.sum(outer_g[...], axis=0)
    tall = jnp.transpose(jnp.concatenate([small, jnp.zeros((channels - 8, channels), F32)], axis=0))
    small_ref[...] = tall[:, :heads]
    gain_out_ref[...] = small[heads : heads + 1]
    both(sums_ref.at[core], s_agc, r_agc)
    await_bytes(x_s.at[pl.ds(0, n_row - 1)], s_fw)
    await_bytes(x_s.at[pl.ds(0, n_row - 1)], s_bw)


def layer(heads, valid_len, pair, cot, gain, bias_rows, projections):
    n_row, n_col = lax.axis_size("row"), lax.axis_size("col")
    tile_rows, tile_cols, channels = pair.shape
    ncols = tile_cols // n_row
    tile = (tile_rows, heads // 2 * tile_cols)
    n_out, n_mates, rows = n_row // 4, 2 * n_col - 1, n_row * tile_rows
    half_out = n_out // 2
    slab = (5 * channels // (4 * n_col), channels)
    vmem = pl.BlockSpec(memory_space=VM)
    peers = (n_row, ncols, tile_rows, channels)
    cols = VM((ncols, n_row, 2, tile_rows, channels), BF16)
    flat = VM((tile_rows * tile_cols, channels), F32)

    def pairs(*shape):
        return [DMA(shape), DMA(shape)]

    return pl.pallas_call(
        functools.partial(layer_kernel, heads),
        in_specs=[pl.BlockSpec(memory_space=pltpu.SMEM)] + [vmem] * 5,
        out_specs=[vmem] * 5,
        out_shape=[
            jax.ShapeDtypeStruct(peers, BF16),
            jax.ShapeDtypeStruct(peers, F32),
            jax.ShapeDtypeStruct((2, 2, n_col) + slab, F32),
            jax.ShapeDtypeStruct((channels, heads), F32),
            jax.ShapeDtypeStruct((1, channels), F32),
        ],
        scratch_shapes=[
            flat, flat, VM((n_row, ncols, 2, tile_rows, channels), BF16),
            VM((2,) + tile, F32),
            VM(pair.shape, F32),
            VM(pair.shape, BF16),
            VM((channels, 4 * channels), BF16),
            cols,
            VM((2, n_out, 2, 2, n_col) + tile, F32),
            VM((heads, rows, rows), F32),
            VM((heads, rows, rows), F32),
            VM((channels, 5 * channels), F32),
            VM((8, channels), F32),
            cols, cols,
            flat,
            VM((2, n_out, 2, n_col) + tile, F32),
            VM((2, 2, n_col, n_out) + tile, BF16),
            VM((2, n_mates, n_out) + tile, BF16),
            VM((2, n_out) + tile, F32),
            VM((2, half_out - 1, 2) + tile, F32),
            VM((2,) + tile, F32),
            VM((2,) + tile, F32),
            VM((2,) + tile, F32),
            VM((2, 2, n_col) + slab, F32),
            VM((2, n_col) + slab, F32),
            VM((2, n_col) + slab, F32),
            VM((n_mates,) + slab, F32),
            VM(slab, F32),
            VM((half_out - 1,) + slab, F32),
            VM(slab, F32),
            VM(slab, F32),
            VM((4 * n_col, 8, channels), F32),
            VM((n_out, 8, channels), F32),
            DMA, DMA((2, ncols)), DMA, DMA((2, ncols)),
            *pairs(2, half_out), *pairs(2, half_out - 1), *pairs(2), *pairs(2, n_col - 1), *pairs(2), DMA((2,)),
            *pairs(3), *pairs(3, n_mates), *pairs(3, 2, half_out - 1), *pairs(3),
            *pairs(n_mates), DMA, DMA, *pairs(4 * n_col - 1), *pairs(n_out - 1),
        ],
        compiler_params=pltpu.CompilerParams(
            collective_id=0, has_side_effects=True, vmem_limit_bytes=63 * 1024 * 1024
        ),
    )(valid_len, pair, cot, gain, bias_rows, projections)


def shards(pair, gain, projections, bias_weight, valid_len, out_cotangent):
    tile_rows, tile_cols, channels = pair.shape
    heads = bias_weight.shape[1]

    def to_tile(columns):
        return jnp.swapaxes(columns.reshape(tile_cols, tile_rows, channels), 0, 1)

    bias_rows = jnp.pad(bias_weight.T, ((0, 8 - heads), (0, 0)))
    attended, pair_gradient, sums, bias_weight_grad, gain_gradient = layer(
        heads, valid_len, pair, out_cotangent, gain[None], bias_rows, projections
    )
    return (
        to_tile(attended),
        to_tile(pair_gradient),
        sums.reshape(5, channels, channels),
        bias_weight_grad,
        gain_gradient[0],
    )


def solution(mesh):
    placed = (P("row", "col", None), P(), P(), P(), P(), P("row", "col", None))
    return jax.shard_map(
        shards,
        mesh=mesh,
        in_specs=placed,
        out_specs=(P("row", "col", None), P("row", "col", None), P(), P(), P()),
        check_vma=False,
    )
```
